128 devices in a mesh: fsdp: 8 (over z, y_hi), ctx: 4 (over y_lo, core), tp: 4 (over x).
Axes of the slice: x: 4, y: 4 (y_hi: 2, y_lo: 2; y = y_hi * 2 + y_lo), z: 4, core: 2. Of those that a mesh axis runs over, the one named last changes fastest.
Arguments:
- hidden_in: bfloat16 [16384, 1024], P(('fsdp', 'ctx', 'tp')), may hold values from -6 to 6
- segment_ids: int32 [8, 2048], P('fsdp'), may hold values from 0 to 3, never falling along the last dimension, each value on 1 to 1024 neighbouring positions
- norm_gain: float32 [1, 2, 1024], P(None, None, ('fsdp', 'ctx', 'tp')), may hold values from 0.5 to 1.5
- norm_bias: float32 [1, 2, 1024], P(None, None, ('fsdp', 'ctx', 'tp')), may hold values from -3 to 3
- w_qkv: bfloat16 [1, 3, 1024, 1024], P(None, None, ('fsdp', 'ctx'), 'tp'), may hold values from -3 to 3
- qv_bias: bfloat16 [1, 2, 16, 64], P(None, None, 'tp', ('fsdp', 'ctx')), may hold values from -3 to 3
- w_out: bfloat16 [1, 1024, 1024], P(None, ('fsdp', 'ctx'), 'tp'), may hold values from -0.5 to 0.5
- out_bias: float32 [1, 2, 1024], P(None, None, ('fsdp', 'ctx', 'tp')), may hold values from -3 to 3
- w_up: bfloat16 [1, 1024, 4096], P(None, ('fsdp', 'ctx'), 'tp'), may hold values from -0.1875 to 0.1875
- up_bias: bfloat16 [1, 16, 256], P(None, 'tp', ('fsdp', 'ctx')), may hold values from -3 to 3
- w_down: bfloat16 [1, 1024, 4096], P(None, ('fsdp', 'ctx'), 'tp'), may hold values from -0.09375 to 0.09375
- cotangent: float32 [16384, 1024], P(('fsdp', 'ctx', 'tp')), may hold values from -6 to 6
Outputs:
- hidden_out: float32 [16384, 1024], P(('fsdp', 'ctx', 'tp'))
- hidden_grad: float32 [16384, 1024], P(('fsdp', 'ctx', 'tp'))
- norm_gain_grad: float32 [1, 2, 1024], P(None, None, ('fsdp', 'ctx', 'tp'))
- norm_bias_grad: float32 [1, 2, 1024], P(None, None, ('fsdp', 'ctx', 'tp'))
- w_qkv_grad: float32 [1, 3, 1024, 1024], P(None, None, ('fsdp', 'ctx'), 'tp')
- qv_bias_grad: float32 [1, 2, 16, 64], P(None, None, 'tp', ('fsdp', 'ctx'))
- w_out_grad: float32 [1, 1024, 1024], P(None, ('fsdp', 'ctx'), 'tp')
- out_bias_grad: float32 [1, 2, 1024], P(None, None, ('fsdp', 'ctx', 'tp'))
- w_up_grad: float32 [1, 1024, 4096], P(None, ('fsdp', 'ctx'), 'tp')
- up_bias_grad: float32 [1, 16, 256], P(None, 'tp', ('fsdp', 'ctx'))
- w_down_grad: float32 [1, 1024, 4096], P(None, ('fsdp', 'ctx'), 'tp')
The draws below stay inside these ranges and needn't reach their ends.
Inputs may be any that keep to these rules, and one draw needn't show every extreme that they name: `segment_ids`: in each group's row the ids never fall; each of the 4 sequences holds 1 to 1024 positions and one holds exactly 1024.
All inputs are finite; a program needn't handle non-finite values.
Results may differ from the reference program's by a relative error of at most 0.025.
Values may be sent and summed in bfloat16 or wider, within the bound.
A program may use at most 128 MiB of HBM per device.

```python
import math
import jax
import jax.numpy as jnp
import numpy as np
from jax import lax

D = 1024
H = 16
HD = 64
FF = 4096
LAYERS = 1
GROUP_TOK = 2048
TOKENS = 16384
SEQS = 4
MAXLEN = 1024
N_FSDP = 8


def draw_w_qkv(key, part):
    normal_key = jax.random.fold_in(jax.random.fold_in(key, 11), 0)
    drawn = jax.random.truncated_normal(normal_key, -4.0, 4.0, (LAYERS, 3, D, D), jnp.float32) * (1.0 / D ** 0.5)
    return jnp.clip(drawn, -3.0, 3.0).astype(jnp.bfloat16)


def levels(rng, shape, shards, least, largest):
    def one(position, shards_of):
        steps = jax.random.uniform(jax.random.fold_in(jax.random.fold_in(rng, 6), position), (shards_of,), jnp.float32, least / len(shards), largest / len(shards))
        return jnp.repeat(jnp.exp(steps), shape[position] // shards_of).reshape((-1,) + (1,) * (len(shape) - position - 1))

    level = one(*shards[0])
    for cut in shards[1:]:
        level = level * one(*cut)
    return level


def split_up(count, total, reach, slope):
    loads = [(1 << 20) // math.isqrt(standing ** slope) + 1 for standing in range(2, count + 1)]
    spare, counts = total - reach - (count - 1), [1] * (count - 1)
    while spare > 0:
        movable = [i for i in range(count - 1) if counts[i] < reach]
        pool, budget = sum([loads[i] for i in movable]), spare
        for i in movable:
            extra = min(reach - counts[i], max(1, budget * loads[i] // pool), spare)
            counts[i] = counts[i] + extra
            spare = spare - extra
    return np.array([reach] + counts)


def ragged_sizes(rng, amount, total, most, skew):
    if amount == 2:
        one = jax.random.randint(rng, (), max(1, total - most), min(most, total - 1) + 1)
        return jnp.stack([one, total - one])
    tallies = jnp.asarray(split_up(amount, total, most, skew), jnp.int32)
    twos = (amount - 1) // 2
    donor, receiver = tallies[1:1 + 2 * twos:2], tallies[2:2 + 2 * twos:2]
    room = jnp.minimum(donor - 1, most - receiver)
    moved = jax.random.randint(jax.random.fold_in(rng, 1), (twos,), 0, 1 << 20) % (room + 1)
    tallies = tallies.at[1:1 + 2 * twos:2].set(donor - moved).at[2:2 + 2 * twos:2].set(receiver + moved)
    return tallies[jax.random.permutation(jax.random.fold_in(rng, 2), amount)]


def gaussian(stream_key, extent, deviation, most, cuts=(), kind=jnp.bfloat16):
    entries = deviation * jax.random.normal(stream_key, extent, jnp.float32)
    if cuts:
        entries = entries * levels(stream_key, extent, cuts, -0.22, 0.18)
    return jnp.clip(entries, -most, most).astype(kind)


def setup_inputs(seed: int = 0) -> dict:
    splits = jax.random.split(jax.random.key(seed), 13)
    return {
        "hidden_in": gaussian(splits[0], (TOKENS, D), 1.0, 6.0, ((0, 128),)),
        "segment_ids": jax.vmap(lambda own: jnp.searchsorted(jnp.cumsum(ragged_sizes(own, SEQS, GROUP_TOK, MAXLEN, 2)), jnp.arange(GROUP_TOK), side="right"))(jax.random.split(splits[1], N_FSDP)).reshape((N_FSDP, GROUP_TOK)).astype(jnp.int32),
        "norm_gain": jnp.clip(1.0 + 0.1 * jax.random.normal(splits[2], (LAYERS, 2, D), jnp.float32), 0.5, 1.5),
        "norm_bias": gaussian(splits[3], (LAYERS, 2, D), 0.5, 3.0, ((2, 128),), jnp.float32),
        "w_qkv": draw_w_qkv(jax.random.fold_in(splits[12], 71), 0),
        "qv_bias": gaussian(splits[5], (LAYERS, 2, H, HD), 0.5, 3.0, ((2, 4), (3, 32))),
        "w_out": gaussian(splits[6], (LAYERS, D, D), (D // 8) ** -0.5, 0.5, ((1, 32), (2, 4))),
        "out_bias": gaussian(splits[7], (LAYERS, 2, D), 0.5, 3.0, ((2, 128),), jnp.float32),
        "w_up": gaussian(splits[8], (LAYERS, D, FF), D ** -0.5, 0.1875, ((1, 32), (2, 4))),
        "up_bias": gaussian(splits[9], (LAYERS, H, FF // H), 0.5, 3.0, ((1, 4), (2, 32))),
        "w_down": gaussian(splits[10], (LAYERS, D, FF), FF ** -0.5, 0.09375, ((1, 32), (2, 4))),
        "cotangent": gaussian(splits[11], (TOKENS, D), 1.0, 6.0, ((0, 128),), jnp.float32),
    }


EPS = 1e-05
ROOT = 0.7978845608028654
CUBIC = 0.044715

def rounded(values_in):
    return lax.optimization_barrier(values_in.astype(jnp.bfloat16)).astype(jnp.float32)

def normalize(residual, norm_gain, norm_shift):
    average = lax.optimization_barrier(jnp.mean(residual, axis=1, keepdims=True))
    centered = residual - average
    inv_std = lax.rsqrt(lax.optimization_barrier(jnp.mean(centered * centered, axis=1, keepdims=True)) + EPS)
    standard = centered * inv_std
    return (standard, inv_std, (standard * norm_gain + norm_shift).astype(jnp.bfloat16))

def normalize_back(grad_norm, standard, inv_std, norm_gain):
    scaled = grad_norm * norm_gain
    return inv_std * (scaled - lax.optimization_barrier(jnp.mean(scaled, axis=1, keepdims=True)) - standard * lax.optimization_barrier(jnp.mean(scaled * standard, axis=1, keepdims=True)))

def gelu_pair(preact):
    curve = jnp.tanh(ROOT * (preact + CUBIC * preact * preact * preact))
    output = 0.5 * preact * (1.0 + curve)
    derivative = 0.5 * (1.0 + curve) + 0.5 * preact * (1.0 - curve * curve) * ROOT * (1.0 + 3.0 * CUBIC * preact * preact)
    return (output, derivative)

def block_scores(queries, keys_all, segments, slopes, first_row, height):
    scores = jnp.einsum('qhd,khd->hqk', queries.astype(jnp.float32), keys_all.astype(jnp.float32)) * (1.0 / math.sqrt(queries.shape[2]))
    row_pos = first_row + jnp.arange(height, dtype=jnp.int32)
    col_pos = jnp.arange(keys_all.shape[0], dtype=jnp.int32)
    distance = (row_pos[:, None] - col_pos[None, :]).astype(jnp.float32)
    row_seg = lax.dynamic_slice_in_dim(segments, first_row, height, 0)
    allowed = (row_pos[:, None] >= col_pos[None, :]) & (row_seg[:, None] == segments[None, :])
    scores = scores - slopes[:, None, None] * distance[None, :, :]
    return jnp.where(allowed[None, :, :], scores, -jnp.inf)

def group_forward(queries, keys_all, values_all, segments, slopes):
    total_rows = queries.shape[0]
    height = min(512, total_rows)

    def one_block(block_index):
        first_row = block_index * height
        block_q = lax.dynamic_slice_in_dim(queries, first_row, height, 0)
        scores = block_scores(block_q, keys_all, segments, slopes, first_row, height)
        highest = lax.optimization_barrier(jnp.max(scores, axis=2, keepdims=True))
        exponent = jnp.exp(scores - highest)
        totals = lax.optimization_barrier(jnp.sum(exponent, axis=2, keepdims=True))
        attention = rounded(exponent / totals)
        mixed = jnp.einsum('hqk,khd->qhd', attention, values_all.astype(jnp.float32)).astype(jnp.bfloat16)
        return (mixed, (highest + jnp.log(totals))[:, :, 0])
    mixed, log_sums = lax.map(one_block, jnp.arange(total_rows // height, dtype=jnp.int32))
    return (mixed.reshape(queries.shape), log_sums)

def group_backward(queries, keys_all, values_all, grad_mixed, log_sums, segments, slopes):
    total_rows = queries.shape[0]
    height = min(512, total_rows)
    scale = 1.0 / math.sqrt(queries.shape[2])

    def one_block(carry, block_index):
        grad_keys, grad_values = carry
        first_row = block_index * height
        block_q = lax.dynamic_slice_in_dim(queries, first_row, height, 0)
        block_g = lax.dynamic_slice_in_dim(grad_mixed, first_row, height, 0)
        scores = block_scores(block_q, keys_all, segments, slopes, first_row, height)
        attention = jnp.exp(scores - log_sums[block_index][:, :, None])
        grad_values = grad_values + jnp.einsum('hqk,qhd->khd', rounded(attention), block_g.astype(jnp.float32))
        grad_attn = jnp.einsum('qhd,khd->hqk', block_g.astype(jnp.float32), values_all.astype(jnp.float32))
        centre = lax.optimization_barrier(jnp.sum(attention * grad_attn, axis=2, keepdims=True))
        grad_scores = rounded(attention * (grad_attn - centre) * scale)
        grad_query = jnp.einsum('hqk,khd->qhd', grad_scores, keys_all.astype(jnp.float32)).astype(jnp.bfloat16)
        grad_keys = grad_keys + jnp.einsum('hqk,qhd->khd', grad_scores, block_q.astype(jnp.float32))
        return ((grad_keys, grad_values), grad_query)
    zeros_init = jnp.zeros(queries.shape, jnp.float32)
    (grad_keys, grad_values), grad_query = lax.scan(one_block, (zeros_init, zeros_init), jnp.arange(total_rows // height, dtype=jnp.int32))
    return (grad_query.reshape(queries.shape), grad_keys.astype(jnp.bfloat16), grad_values.astype(jnp.bfloat16))

def reference(hidden_in, segment_ids, norm_gain, norm_bias, w_qkv, qv_bias, w_out, out_bias, w_up, up_bias, w_down, cotangent):
    slopes = jnp.exp2(-8.0 * (jnp.arange(H, dtype=jnp.int32) + 1).astype(jnp.float32) / H)
    split = (N_FSDP, GROUP_TOK, H, HD)

    def forward_group(packed):
        return group_forward(packed[0], packed[1], packed[2], packed[3], slopes)

    def backward_group(packed):
        return group_backward(packed[0], packed[1], packed[2], packed[3], packed[4], packed[5], slopes)
    residual = hidden_in.astype(jnp.float32)
    stored = []
    for layer_index in range(LAYERS):
        standard_attn, inv_attn, normed_attn = normalize(residual, norm_gain[layer_index, 0], norm_bias[layer_index, 0])
        qv_add = qv_bias[layer_index].astype(jnp.float32).reshape(2, D)
        queries = (jnp.dot(normed_attn, w_qkv[layer_index, 0], preferred_element_type=jnp.float32) + qv_add[0]).astype(jnp.bfloat16)
        keys_all = jnp.dot(normed_attn, w_qkv[layer_index, 1], preferred_element_type=jnp.float32).astype(jnp.bfloat16)
        values_all = (jnp.dot(normed_attn, w_qkv[layer_index, 2], preferred_element_type=jnp.float32) + qv_add[1]).astype(jnp.bfloat16)
        mixed, log_sums = lax.map(forward_group, (queries.reshape(split), keys_all.reshape(split), values_all.reshape(split), segment_ids))
        mixed = mixed.reshape(TOKENS, D)
        residual_mid = residual + jnp.dot(mixed, w_out[layer_index].T, preferred_element_type=jnp.float32) + out_bias[layer_index, 0]
        standard_mlp, inv_mlp, normed_mlp = normalize(residual_mid, norm_gain[layer_index, 1], norm_bias[layer_index, 1])
        preact = jnp.dot(normed_mlp, w_up[layer_index], preferred_element_type=jnp.float32) + up_bias[layer_index].astype(jnp.float32).reshape(FF)
        activated, derivative = gelu_pair(preact)
        activated = activated.astype(jnp.bfloat16)
        residual = residual_mid + jnp.dot(activated, w_down[layer_index].T, preferred_element_type=jnp.float32) + out_bias[layer_index, 1]
        stored.append((standard_attn, inv_attn, normed_attn, queries, keys_all, values_all, log_sums, mixed, standard_mlp, inv_mlp, normed_mlp, derivative, activated))
    final_out = residual
    gradient = cotangent
    results = [None] * LAYERS
    for layer_index in reversed(range(LAYERS)):
        standard_attn, inv_attn, normed_attn, queries, keys_all, values_all, log_sums, mixed, standard_mlp, inv_mlp, normed_mlp, derivative, activated = stored[layer_index]
        down_bias_grad = lax.optimization_barrier(jnp.sum(gradient, axis=0))
        grad_out16 = gradient.astype(jnp.bfloat16)
        grad_down = jnp.dot(grad_out16.T, activated, preferred_element_type=jnp.float32)
        grad_pre = jnp.dot(grad_out16, w_down[layer_index], preferred_element_type=jnp.float32) * derivative
        up_bias_grad = lax.optimization_barrier(jnp.sum(grad_pre, axis=0)).reshape(H, FF // H)
        grad_pre16 = grad_pre.astype(jnp.bfloat16)
        grad_up = jnp.dot(normed_mlp.T, grad_pre16, preferred_element_type=jnp.float32)
        grad_norm = jnp.dot(grad_pre16, w_up[layer_index].T, preferred_element_type=jnp.float32)
        gain_mlp = lax.optimization_barrier(jnp.sum(grad_norm * standard_mlp, axis=0))
        shift_mlp = lax.optimization_barrier(jnp.sum(grad_norm, axis=0))
        grad_mid = gradient + normalize_back(grad_norm, standard_mlp, inv_mlp, norm_gain[layer_index, 1])
        attn_bias_grad = lax.optimization_barrier(jnp.sum(grad_mid, axis=0))
        grad_attn16 = grad_mid.astype(jnp.bfloat16)
        grad_wout = jnp.dot(grad_attn16.T, mixed, preferred_element_type=jnp.float32)
        grad_mixed = jnp.dot(grad_attn16, w_out[layer_index], preferred_element_type=jnp.float32).astype(jnp.bfloat16)
        grad_q, grad_k, grad_v = lax.map(backward_group, (queries.reshape(split), keys_all.reshape(split), values_all.reshape(split), grad_mixed.reshape(split), log_sums, segment_ids))
        grad_q = grad_q.reshape(TOKENS, D)
        grad_k = grad_k.reshape(TOKENS, D)
        grad_v = grad_v.reshape(TOKENS, D)
        qv_grad = jnp.stack([lax.optimization_barrier(jnp.sum(grad_q.astype(jnp.float32), axis=0)), lax.optimization_barrier(jnp.sum(grad_v.astype(jnp.float32), axis=0))]).reshape(2, H, HD)
        grad_qkv = jnp.stack([jnp.dot(normed_attn.T, grad_q, preferred_element_type=jnp.float32), jnp.dot(normed_attn.T, grad_k, preferred_element_type=jnp.float32), jnp.dot(normed_attn.T, grad_v, preferred_element_type=jnp.float32)])
        grad_norm = jnp.dot(grad_q, w_qkv[layer_index, 0].T, preferred_element_type=jnp.float32) + jnp.dot(grad_k, w_qkv[layer_index, 1].T, preferred_element_type=jnp.float32) + jnp.dot(grad_v, w_qkv[layer_index, 2].T, preferred_element_type=jnp.float32)
        gain_attn = lax.optimization_barrier(jnp.sum(grad_norm * standard_attn, axis=0))
        shift_attn = lax.optimization_barrier(jnp.sum(grad_norm, axis=0))
        gradient = grad_mid + normalize_back(grad_norm, standard_attn, inv_attn, norm_gain[layer_index, 0])
        results[layer_index] = (jnp.stack([gain_attn, gain_mlp]), jnp.stack([shift_attn, shift_mlp]), grad_qkv, qv_grad, grad_wout, jnp.stack([attn_bias_grad, down_bias_grad]), grad_up, up_bias_grad, grad_down)
    stacked = [jnp.stack([results[layer_index][member] for layer_index in range(LAYERS)]) for member in range(9)]
    return (final_out, gradient, stacked[0], stacked[1], stacked[2], stacked[3], stacked[4], stacked[5], stacked[6], stacked[7], stacked[8])
```

```python
import functools
import math

import jax
import jax.numpy as jnp
from jax import lax
from jax.experimental import pallas as pl
from jax.experimental.pallas import tpu as pltpu
from jax.sharding import PartitionSpec as P

H = 16
HD = 64
EPS = 1e-05
ROOT = 0.7978845608028654
CUBIC = 0.044715
CONTRACT_ROWS = (((0,), (0,)), ((), ()))
CONTRACT_COLS = (((1,), (1,)), ((), ()))
MESH = pl.DeviceIdType.MESH
F32 = jnp.float32
BF16 = jnp.bfloat16

COLS = 3072
QKV = slice(0, 768)
OUT = slice(768, 1024)
UP = slice(1024, 2048)
DOWN = slice(2048, 3072)


def normalize(residual, norm_gain, norm_shift):
    average = jnp.mean(residual, axis=1, keepdims=True)
    centered = residual - average
    inv_std = lax.rsqrt(jnp.mean(centered * centered, axis=1, keepdims=True) + EPS)
    standard = centered * inv_std
    return (standard, inv_std, (standard * norm_gain + norm_shift).astype(BF16))


def normalize_back(grad_norm, standard, inv_std, norm_gain):
    scaled = grad_norm * norm_gain
    return inv_std * (
        scaled
        - jnp.mean(scaled, axis=1, keepdims=True)
        - standard * jnp.mean(scaled * standard, axis=1, keepdims=True)
    )


def gelu_pair(preact):
    curve = jnp.tanh(ROOT * (preact + CUBIC * preact * preact * preact))
    output = 0.5 * preact * (1.0 + curve)
    derivative = 0.5 * (1.0 + curve) + 0.5 * preact * (1.0 - curve * curve) * ROOT * (
        1.0 + 3.0 * CUBIC * preact * preact
    )
    return (output, derivative)


def place():
    f = lax.axis_index("fsdp")
    k = lax.axis_index("ctx")
    t = lax.axis_index("tp")
    return f // 2, lax.rem(f, 2) * 2 + k // 2, lax.rem(k, 2), t


def device(z, y, c, t):
    return (z * 2 + y // 2, lax.rem(y, 2) * 2 + c, t)


def around(index, step):
    return lax.rem(index + step, 4)


def greet(partners):
    barrier = pltpu.get_barrier_semaphore()
    for partner in partners:
        pl.semaphore_signal(barrier, inc=1, device_id=partner, device_id_type=MESH)
    pl.semaphore_wait(barrier, len(partners))


def all_partners(z, y, c, t):
    return (
        [device(z, around(y, d), c, t) for d in (1, 2, 3)]
        + [device(around(z, d), y, c, t) for d in (1, 2, 3)]
        + [device(z, y, c, around(t, d)) for d in (1, 2, 3)]
        + [device(z, y, 1 - c, t)]
    )


class Copies:
    def __init__(self, send_sems, recv_sems):
        self.send_sems, self.recv_sems, self.used, self.all = send_sems, recv_sems, 0, []

    def make(self, src, dst, target):
        index = self.used
        self.used += 1
        copy = pltpu.make_async_remote_copy(
            src_ref=src,
            dst_ref=dst,
            send_sem=self.send_sems.at[index],
            recv_sem=self.recv_sems.at[index],
            device_id=target,
            device_id_type=MESH,
        )
        copy.start()
        self.all.append(copy)
        return copy

    def finish(self):
        for copy in self.all:
            copy.wait_send()


GATHER_GROUPS = (slice(0, 768), slice(768, 3072))


def gather_kernel(slab, small, whole, params, send_sems, recv_sems, local_sem):
    z, y, c, t = place()
    greet(all_partners(z, y, c, t))
    copies = Copies(send_sems, recv_sems)
    steps = (1, 2, 3)

    params[t, z, y, c] = small[...]
    small_x = [
        copies.make(params.at[t, z, y, c], params.at[t, z, y, c], device(z, y, c, around(t, d)))
        for d in steps
    ]
    local = pltpu.make_async_copy(slab, whole.at[z, y, c], local_sem)
    local.start()
    first = []
    for cols in GATHER_GROUPS:
        from_y = [
            copies.make(
                slab.at[:, cols], whole.at[z, y, c, :, cols], device(z, around(y, d), c, t)
            )
            for d in steps
        ]
        from_z = [
            copies.make(
                slab.at[:, cols], whole.at[z, y, c, :, cols], device(around(z, d), y, c, t)
            )
            for d in steps
        ]
        first.append((from_y, from_z))
    for copy in small_x:
        copy.wait_recv()
    small_y = [
        copies.make(params.at[:, z, y, c], params.at[:, z, y, c], device(z, around(y, d), c, t))
        for d in steps
    ]
    local.wait()
    small_z = None
    second = []
    for cols, (from_y, from_z) in zip(GATHER_GROUPS, first):
        upper, lower = pl.ds(0, 16), pl.ds(16, 16)
        via_y = [[None] * 3 for _ in steps]
        via_z = [[None] * 3 for _ in steps]
        for d in steps:
            from_y[d - 1].wait_recv()
            piece = whole.at[z, around(y, 4 - d), c, upper, cols]
            for e in steps:
                via_y[e - 1][d - 1] = copies.make(piece, piece, device(around(z, e), y, c, t))
            from_z[d - 1].wait_recv()
            piece = whole.at[around(z, 4 - d), y, c, lower, cols]
            for e in steps:
                via_z[d - 1][e - 1] = copies.make(piece, piece, device(z, around(y, e), c, t))
        block = whole.at[z, :, c, :, cols]
        core = [copies.make(block, block, device(z, y, 1 - c, t))]
        second.append((via_y, via_z, core))
        if small_z is None:
            for copy in small_y:
                copy.wait_recv()
            small_z = [
                copies.make(
                    params.at[:, z, :, c], params.at[:, z, :, c], device(around(z, d), y, c, t)
                )
                for d in steps
            ]
    small_c = None
    for cols, (via_y, via_z, core) in zip(GATHER_GROUPS, second):
        for e in steps:
            for d in steps:
                via_y[e - 1][d - 1].wait_recv()
                via_z[e - 1][d - 1].wait_recv()
            block = whole.at[around(z, 4 - e), :, c, :, cols]
            core.append(copies.make(block, block, device(z, y, 1 - c, t)))
        if small_c is None:
            for copy in small_z:
                copy.wait_recv()
            small_c = copies.make(
                params.at[:, :, :, c], params.at[:, :, :, c], device(z, y, 1 - c, t)
            )
    for _, _, core in second:
        for copy in core:
            copy.wait_recv()
    small_c.wait_recv()
    copies.finish()


def gather_weights(slab, small):
    count = 10 + 2 * (6 + 18 + 4)
    return pl.pallas_call(
        gather_kernel,
        out_shape=(
            jax.ShapeDtypeStruct((4, 4, 2, 32, COLS), BF16),
            jax.ShapeDtypeStruct((4, 4, 4, 2, 1, 128), F32),
        ),
        in_specs=[
            pl.BlockSpec(memory_space=pltpu.VMEM),
            pl.BlockSpec(memory_space=pltpu.VMEM),
        ],
        out_specs=(
            pl.BlockSpec(memory_space=pl.ANY),
            pl.BlockSpec(memory_space=pltpu.VMEM),
        ),
        scratch_shapes=[
            pltpu.SemaphoreType.DMA((count,)),
            pltpu.SemaphoreType.DMA((count,)),
            pltpu.SemaphoreType.DMA,
        ],
        compiler_params=pltpu.CompilerParams(
            collective_id=0, has_side_effects=True, vmem_limit_bytes=8 << 20
        ),
        name="gather_weights",
    )(slab, small)


CHUNKS = 4
WIDTH = COLS // CHUNKS


def reduce_kernel(
    grads,
    small,
    out,
    small_out,
    own,
    core_in,
    a_in,
    b_in,
    a_sum,
    b_sum,
    a_last,
    b_last,
    x_in,
    x_sum,
    c_in,
    c_sum,
    z_in,
    z_sum,
    y_in,
    send_sems,
    recv_sems,
    local_sems,
):
    z, y, c, t = place()
    greet(all_partners(z, y, c, t))
    copies = Copies(send_sems, recv_sems)
    steps = (1, 2, 3)
    sibling = device(z, y, 1 - c, t)

    core, local = [], []
    for k in range(CHUNKS):
        cols = slice(k * WIDTH, (k + 1) * WIDTH)
        copy = pltpu.make_async_copy(grads.at[:, :, c, :, cols], own.at[k], local_sems.at[k])
        copy.start()
        local.append(copy)
        core.append(copies.make(grads.at[:, :, 1 - c, :, cols], core_in.at[k], sibling))
    small_x = [
        copies.make(small.at[around(t, d)], x_in.at[d - 1], device(z, y, c, around(t, d)))
        for d in steps
    ]
    a_first, b_first = [], []
    small_c = None
    for k in range(CHUNKS):
        local[k].wait()
        core[k].wait_recv()

        def add(i, carry):
            zz, yy = i // 4, lax.rem(i, 4)
            total = own[k, zz, yy].astype(F32) + core_in[k, zz, yy].astype(F32)
            own[k, zz, yy] = total.astype(BF16)
            return carry

        lax.fori_loop(0, 16, add, 0)
        a_first.append(
            [
                copies.make(
                    own.at[k, around(z, d), :, pl.ds(0, 16)],
                    a_in.at[k, d - 1],
                    device(around(z, d), y, c, t),
                )
                for d in steps
            ]
        )
        b_first.append(
            [
                copies.make(
                    own.at[k, :, around(y, d), pl.ds(16, 16)],
                    b_in.at[k, d - 1],
                    device(z, around(y, d), c, t),
                )
                for d in steps
            ]
        )
        if small_c is None:
            for copy in small_x:
                copy.wait_recv()
            x_sum[...] = small[t] + x_in[0] + x_in[1] + x_in[2]
            small_c = copies.make(x_sum.at[:, :, 1 - c], c_in, sibling)
    a_second, b_second = [], []
    small_z = None
    for k in range(CHUNKS):
        for copy in a_first[k]:
            copy.wait_recv()

        def add_a(i, carry):
            total = own[k, z, i, 0:16].astype(F32)
            for d in range(3):
                total = total + a_in[k, d, i].astype(F32)
            a_sum[k, i] = total.astype(BF16)
            return carry

        lax.fori_loop(0, 4, add_a, 0)
        a_second.append(
            [
                copies.make(
                    a_sum.at[k, around(y, d)], a_last.at[k, d - 1], device(z, around(y, d), c, t)
                )
                for d in steps
            ]
        )
        for copy in b_first[k]:
            copy.wait_recv()

        def add_b(i, carry):
            total = own[k, i, y, 16:32].astype(F32)
            for d in range(3):
                total = total + b_in[k, d, i].astype(F32)
            b_sum[k, i] = total.astype(BF16)
            return carry

        lax.fori_loop(0, 4, add_b, 0)
        b_second.append(
            [
                copies.make(
                    b_sum.at[k, around(z, d)], b_last.at[k, d - 1], device(around(z, d), y, c, t)
                )
                for d in steps
            ]
        )
        if small_z is None:
            small_c.wait_recv()
            c_sum[...] = x_sum[:, :, c] + c_in[...]
            small_z = [
                copies.make(c_sum.at[around(z, d)], z_in.at[d - 1], device(around(z, d), y, c, t))
                for d in steps
            ]
    for copy in small_z:
        copy.wait_recv()
    z_sum[...] = c_sum[z] + z_in[0] + z_in[1] + z_in[2]
    small_y = [
        copies.make(z_sum.at[around(y, d)], y_in.at[d - 1], device(z, around(y, d), c, t))
        for d in steps
    ]
    for k in range(CHUNKS):
        cols = slice(k * WIDTH, (k + 1) * WIDTH)
        for copy in a_second[k]:
            copy.wait_recv()
        total = a_sum[k, y].astype(F32)
        for d in range(3):
            total = total + a_last[k, d].astype(F32)
        out[0:16, cols] = total
        for copy in b_second[k]:
            copy.wait_recv()
        total = b_sum[k, z].astype(F32)
        for d in range(3):
            total = total + b_last[k, d].astype(F32)
        out[16:32, cols] = total
    for copy in small_y:
        copy.wait_recv()
    small_out[...] = z_sum[y] + y_in[0] + y_in[1] + y_in[2]
    copies.finish()


def reduce_grads(grads, small):
    count = 10 + CHUNKS * 13
    return pl.pallas_call(
        reduce_kernel,
        out_shape=(
            jax.ShapeDtypeStruct((32, COLS), F32),
            jax.ShapeDtypeStruct((1, 128), F32),
        ),
        in_specs=[
            pl.BlockSpec(memory_space=pl.ANY),
            pl.BlockSpec(memory_space=pltpu.VMEM),
        ],
        out_specs=(
            pl.BlockSpec(memory_space=pltpu.VMEM),
            pl.BlockSpec(memory_space=pltpu.VMEM),
        ),
        scratch_shapes=[
            pltpu.VMEM((CHUNKS, 4, 4, 32, WIDTH), BF16),
            pltpu.VMEM((CHUNKS, 4, 4, 32, WIDTH), BF16),
            pltpu.VMEM((CHUNKS, 3, 4, 16, WIDTH), BF16),
            pltpu.VMEM((CHUNKS, 3, 4, 16, WIDTH), BF16),
            pltpu.VMEM((CHUNKS, 4, 16, WIDTH), BF16),
            pltpu.VMEM((CHUNKS, 4, 16, WIDTH), BF16),
            pltpu.VMEM((CHUNKS, 3, 16, WIDTH), BF16),
            pltpu.VMEM((CHUNKS, 3, 16, WIDTH), BF16),
            pltpu.VMEM((3, 4, 4, 2, 1, 128), F32),
            pltpu.VMEM((4, 4, 2, 1, 128), F32),
            pltpu.VMEM((4, 4, 1, 128), F32),
            pltpu.VMEM((4, 4, 1, 128), F32),
            pltpu.VMEM((3, 4, 1, 128), F32),
            pltpu.VMEM((4, 1, 128), F32),
            pltpu.VMEM((3, 1, 128), F32),
            pltpu.SemaphoreType.DMA((count,)),
            pltpu.SemaphoreType.DMA((count,)),
            pltpu.SemaphoreType.DMA((CHUNKS,)),
        ],
        compiler_params=pltpu.CompilerParams(
            collective_id=1, has_side_effects=True, vmem_limit_bytes=32 << 20
        ),
        name="reduce_grads",
    )(grads, small)


def block_height(total_rows):
    return min(total_rows, max(512, total_rows // 8))


def key_window(first_row, height, total_rows):
    longest = min(2048, total_rows // 2)
    start = max(0, first_row - longest + 1) // 128 * 128
    return (start, first_row + height)


def block_scores(block_q, keys_part, segments, slope, first_row, key_first):
    height = block_q.shape[0]
    width = keys_part.shape[0]
    scores = lax.dot_general(block_q, keys_part, CONTRACT_COLS, preferred_element_type=F32) * (
        1.0 / math.sqrt(HD)
    )
    row_pos = first_row + jnp.arange(height, dtype=jnp.int32)
    col_pos = key_first + jnp.arange(width, dtype=jnp.int32)
    distance = (row_pos[:, None] - col_pos[None, :]).astype(F32)
    row_seg = segments[first_row : first_row + height]
    col_seg = segments[key_first : key_first + width]
    allowed = (row_pos[:, None] >= col_pos[None, :]) & (row_seg[:, None] == col_seg[None, :])
    scores = scores - slope * distance
    return jnp.where(allowed, scores, -jnp.inf)


def attend(queries, keys_all, values_all, segments, slope):
    total_rows = queries.shape[0]
    height = block_height(total_rows)
    outputs = []
    sums = []
    for block_index in range(total_rows // height):
        first_row = block_index * height
        key_first, key_end = key_window(first_row, height, total_rows)
        block_q = queries[first_row : first_row + height]
        scores = block_scores(
            block_q, keys_all[key_first:key_end], segments, slope, first_row, key_first
        )
        highest = jnp.max(scores, axis=1, keepdims=True)
        exponent = jnp.exp(scores - highest)
        totals = jnp.sum(exponent, axis=1, keepdims=True)
        attention = (exponent / totals).astype(BF16)
        outputs.append(
            jnp.dot(attention, values_all[key_first:key_end], preferred_element_type=F32).astype(
                BF16
            )
        )
        sums.append(highest + jnp.log(totals))
    return (jnp.concatenate(outputs, axis=0), sums)


def attend_back(queries, keys_all, values_all, grad_mixed, log_sums, segments, slope):
    total_rows = queries.shape[0]
    height = block_height(total_rows)
    scale = 1.0 / math.sqrt(HD)
    grad_keys = jnp.zeros(queries.shape, F32)
    grad_values = jnp.zeros(queries.shape, F32)
    query_parts = []
    for block_index in range(total_rows // height):
        first_row = block_index * height
        key_first, key_end = key_window(first_row, height, total_rows)
        block_q = queries[first_row : first_row + height]
        block_g = grad_mixed[first_row : first_row + height]
        keys_part = keys_all[key_first:key_end]
        values_part = values_all[key_first:key_end]
        scores = block_scores(block_q, keys_part, segments, slope, first_row, key_first)
        attention = jnp.exp(scores - log_sums[block_index])
        grad_values = grad_values.at[key_first:key_end].add(
            lax.dot_general(
                attention.astype(BF16), block_g, CONTRACT_ROWS, preferred_element_type=F32
            )
        )
        grad_attn = lax.dot_general(
            block_g, values_part, CONTRACT_COLS, preferred_element_type=F32
        )
        centre = jnp.sum(attention * grad_attn, axis=1, keepdims=True)
        grad_scores = (attention * (grad_attn - centre) * scale).astype(BF16)
        query_parts.append(
            jnp.dot(grad_scores, keys_part, preferred_element_type=F32).astype(BF16)
        )
        grad_keys = grad_keys.at[key_first:key_end].add(
            lax.dot_general(grad_scores, block_q, CONTRACT_ROWS, preferred_element_type=F32)
        )
    return (
        jnp.concatenate(query_parts, axis=0),
        grad_keys.astype(BF16),
        grad_values.astype(BF16),
    )


def rows_all(local_rows):
    rows, width = local_rows.shape
    copies = jnp.broadcast_to(local_rows[None], (4, rows, width))
    return lax.all_to_all(copies, "tp", split_axis=0, concat_axis=0, tiled=True).reshape(
        4 * rows, width
    )


def rows_sum(partial_sum):
    rows, width = partial_sum.shape
    parts = partial_sum.astype(BF16).reshape(4, rows // 4, width)
    parts = lax.all_to_all(parts, "tp", split_axis=0, concat_axis=0, tiled=True)
    return jnp.sum(parts.astype(F32), axis=0)


def to_heads(rows):
    return lax.all_to_all(rows, "ctx", split_axis=1, concat_axis=0, tiled=True)


def to_rows(heads):
    return lax.all_to_all(heads, "ctx", split_axis=0, concat_axis=1, tiled=True)


def on_device(
    hidden_in,
    segment_ids,
    norm_gain,
    norm_bias,
    w_qkv,
    qv_bias,
    w_out,
    out_bias,
    w_up,
    up_bias,
    w_down,
    cotangent,
):
    segments = segment_ids[0]
    tp = lax.axis_index("tp")
    head = tp * 4 + lax.axis_index("ctx")
    slope = jnp.exp2(-8.0 * (head + 1).astype(F32) / H)

    qkv_cols = w_qkv[0].reshape(3, 32, 4, 64).transpose(1, 2, 0, 3).reshape(32, 768)
    slab = jnp.concatenate([qkv_cols, w_out[0], w_up[0], w_down[0]], axis=1)
    small = jnp.concatenate(
        [
            norm_gain.reshape(16),
            norm_bias.reshape(16),
            out_bias.reshape(16),
            qv_bias.astype(F32).reshape(16),
            up_bias.astype(F32).reshape(32),
            jnp.zeros((32,), F32),
        ]
    ).reshape(1, 128)
    whole, params = gather_weights(slab, small)
    whole = whole.reshape(1024, COLS)
    params = params.reshape(4, 32, 128)
    wide = params[:, :, 0:48].reshape(4, 32, 3, 2, 8).transpose(2, 3, 1, 0, 4).reshape(3, 2, 1024)
    gains, shifts, biases = wide[0], wide[1], wide[2]
    mine = lax.dynamic_index_in_dim(params, tp, 0, keepdims=False)
    bias_qv = mine[:, 48:64].reshape(32, 2, 4, 2).transpose(1, 2, 0, 3).reshape(2, 4, 64)
    bias_up = mine[:, 64:96].reshape(32, 4, 8).transpose(1, 0, 2).reshape(1024)
    bias_qkv = jnp.stack([bias_qv[0], jnp.zeros((4, 64), F32), bias_qv[1]], axis=1).reshape(768)
    mat_qkv, mat_out, mat_up, mat_down = (
        whole[:, QKV],
        whole[:, OUT],
        whole[:, UP],
        whole[:, DOWN],
    )

    residual = hidden_in.astype(F32)
    standard_attn, inv_attn, normed_attn = normalize(residual, gains[0], shifts[0])
    wide_attn = rows_all(normed_attn)
    grad_wide = rows_all(cotangent.astype(BF16))
    qkv = (jnp.dot(wide_attn, mat_qkv, preferred_element_type=F32) + bias_qkv).astype(BF16)
    heads = to_heads(qkv)
    head_q, head_k, head_v = heads[:, 0:64], heads[:, 64:128], heads[:, 128:192]
    head_out, log_sums = attend(head_q, head_k, head_v, segments, slope)
    mixed = to_rows(head_out)
    residual_mid = (
        residual
        + rows_sum(lax.dot_general(mixed, mat_out, CONTRACT_COLS, preferred_element_type=F32))
        + biases[0]
    )
    standard_mlp, inv_mlp, normed_mlp = normalize(residual_mid, gains[1], shifts[1])
    wide_mlp = rows_all(normed_mlp)
    preact = jnp.dot(wide_mlp, mat_up, preferred_element_type=F32) + bias_up
    activated, derivative = gelu_pair(preact)
    activated = activated.astype(BF16)
    hidden_out = (
        residual_mid
        + rows_sum(lax.dot_general(activated, mat_down, CONTRACT_COLS, preferred_element_type=F32))
        + biases[1]
    )

    gradient = cotangent
    down_bias_grad = jnp.sum(gradient, axis=0)
    grad_pre = jnp.dot(grad_wide, mat_down, preferred_element_type=F32) * derivative
    up_bias_grad = jnp.sum(grad_pre, axis=0)
    grad_pre16 = grad_pre.astype(BF16)
    grad_norm = rows_sum(
        lax.dot_general(grad_pre16, mat_up, CONTRACT_COLS, preferred_element_type=F32)
    )
    grad_down = lax.dot_general(grad_wide, activated, CONTRACT_ROWS, preferred_element_type=F32)
    grad_up = lax.dot_general(wide_mlp, grad_pre16, CONTRACT_ROWS, preferred_element_type=F32)
    gain_mlp = jnp.sum(grad_norm * standard_mlp, axis=0)
    shift_mlp = jnp.sum(grad_norm, axis=0)
    grad_mid = gradient + normalize_back(grad_norm, standard_mlp, inv_mlp, gains[1])
    attn_bias_grad = jnp.sum(grad_mid, axis=0)
    grad_attn = rows_all(grad_mid.astype(BF16))
    grad_wout = lax.dot_general(grad_attn, mixed, CONTRACT_ROWS, preferred_element_type=F32)
    grad_mixed = jnp.dot(grad_attn, mat_out, preferred_element_type=F32).astype(BF16)
    grad_heads = to_heads(grad_mixed)
    grad_q, grad_k, grad_v = attend_back(
        head_q, head_k, head_v, grad_heads, log_sums, segments, slope
    )
    rows_qkv = to_rows(jnp.concatenate([grad_q, grad_k, grad_v], axis=1))
    qkv_sums = jnp.sum(rows_qkv.astype(F32), axis=0).reshape(4, 3, 64)
    grad_qkv = lax.dot_general(wide_attn, rows_qkv, CONTRACT_ROWS, preferred_element_type=F32)
    grad_norm = rows_sum(
        lax.dot_general(rows_qkv, mat_qkv, CONTRACT_COLS, preferred_element_type=F32)
    )
    gain_attn = jnp.sum(grad_norm * standard_attn, axis=0)
    shift_attn = jnp.sum(grad_norm, axis=0)
    grad_input = grad_mid + normalize_back(grad_norm, standard_attn, inv_attn, gains[0])

    grads = jnp.concatenate(
        [
            grad_qkv.astype(BF16),
            grad_wout.astype(BF16),
            grad_up.astype(BF16),
            grad_down.astype(BF16),
        ],
        axis=1,
    ).reshape(4, 4, 2, 32, COLS)
    wide_sums = (
        jnp.stack([gain_attn, gain_mlp, shift_attn, shift_mlp, attn_bias_grad, down_bias_grad])
        .reshape(6, 32, 4, 8)
        .transpose(2, 1, 0, 3)
        .reshape(4, 32, 48)
    )
    qv_sums = (
        jnp.stack([qkv_sums[:, 0], qkv_sums[:, 2]])
        .reshape(2, 4, 32, 2)
        .transpose(2, 0, 1, 3)
        .reshape(32, 16)
    )
    up_sums = up_bias_grad.reshape(4, 32, 8).transpose(1, 0, 2).reshape(32, 32)
    mine_sums = jnp.concatenate([qv_sums, up_sums], axis=1)
    here = (jnp.arange(4) == tp)[:, None, None]
    small_sums = jnp.concatenate(
        [wide_sums, jnp.where(here, mine_sums[None], 0.0), jnp.zeros((4, 32, 32), F32)], axis=2
    ).reshape(4, 4, 4, 2, 1, 128)
    out, small_out = reduce_grads(grads, small_sums)
    flat = small_out.reshape(128)
    return (
        hidden_out,
        grad_input,
        flat[0:16].reshape(1, 2, 8),
        flat[16:32].reshape(1, 2, 8),
        out[:, QKV].reshape(32, 4, 3, 64).transpose(2, 0, 1, 3).reshape(1, 3, 32, 256),
        flat[48:64].reshape(1, 2, 4, 2),
        out[:, OUT].reshape(1, 32, 256),
        flat[32:48].reshape(1, 2, 8),
        out[:, UP].reshape(1, 32, 1024),
        flat[64:96].reshape(1, 4, 8),
        out[:, DOWN].reshape(1, 32, 1024),
    )


def solution(mesh):
    return jax.shard_map(
        on_device,
        mesh=mesh,
        in_specs=(
            P(("fsdp", "ctx", "tp"), None),
            P("fsdp", None),
            P(None, None, ("fsdp", "ctx", "tp")),
            P(None, None, ("fsdp", "ctx", "tp")),
            P(None, None, ("fsdp", "ctx"), "tp"),
            P(None, None, "tp", ("fsdp", "ctx")),
            P(None, ("fsdp", "ctx"), "tp"),
            P(None, None, ("fsdp", "ctx", "tp")),
            P(None, ("fsdp", "ctx"), "tp"),
            P(None, "tp", ("fsdp", "ctx")),
            P(None, ("fsdp", "ctx"), "tp"),
            P(("fsdp", "ctx", "tp"), None),
        ),
        out_specs=(
            P(("fsdp", "ctx", "tp"), None),
            P(("fsdp", "ctx", "tp"), None),
            P(None, None, ("fsdp", "ctx", "tp")),
            P(None, None, ("fsdp", "ctx", "tp")),
            P(None, None, ("fsdp", "ctx"), "tp"),
            P(None, None, "tp", ("fsdp", "ctx")),
            P(None, ("fsdp", "ctx"), "tp"),
            P(None, None, ("fsdp", "ctx", "tp")),
            P(None, ("fsdp", "ctx"), "tp"),
            P(None, "tp", ("fsdp", "ctx")),
            P(None, ("fsdp", "ctx"), "tp"),
        ),
        check_vma=False,
    )
```

```python
import jax
import jax.numpy as jnp
from jax import lax
from jax.experimental import pallas as pl
from jax.experimental.pallas import tpu as pltpu
from jax.sharding import PartitionSpec as P

H = 16
HD = 64
EPS = 1e-05
ROOT = 0.7978845608028654
CUBIC = 0.044715
NN = (((1,), (0,)), ((), ()))
NT = (((1,), (1,)), ((), ()))
TN = (((0,), (0,)), ((), ()))
MESH = pl.DeviceIdType.MESH
F32 = jnp.float32
BF16 = jnp.bfloat16
STEPS = (1, 2, 3)

QKV = slice(0, 768)
UP = slice(768, 1792)
DOWN = slice(1792, 2816)
OUT = slice(2816, 3840)
REST = slice(768, 3840)
WIDE = 3840
SLAB = 3072
CHUNKS = 3
WIDTH = 1024
BLOCK = 256


def around(index, step):
    return lax.rem(index + step, 4)


def dot(a, b, dims=NN):
    return lax.dot_general(a, b, dims, preferred_element_type=F32)


class Copies:
    def __init__(self, send_sems, recv_sems):
        self.send_sems, self.recv_sems, self.used, self.all = send_sems, recv_sems, 0, []

    def make(self, src, dst, target):
        index = self.used
        self.used += 1
        copy = pltpu.make_async_remote_copy(
            src_ref=src,
            dst_ref=dst,
            send_sem=self.send_sems.at[index],
            recv_sem=self.recv_sems.at[index],
            device_id=target,
            device_id_type=MESH,
        )
        copy.start()
        self.all.append(copy)
        return copy

    def finish(self):
        for copy in self.all:
            copy.wait_send()


def arrived(copies):
    for copy in copies:
        copy.wait_recv()


def row_mean(x):
    return jnp.mean(x, axis=1, keepdims=True)


def layer_kernel(
    slab,
    small,
    hidden,
    cot,
    starts,
    slope_ref,
    r2_out,
    g0_out,
    slab_out,
    small_out,
    whole,
    near_c,
    near_x,
    tile_own,
    tile_z,
    pack_y,
    pack_yin,
    vec,
    bias_q,
    bias_u,
    wide1,
    gwide,
    wide2,
    gawide,
    unit1,
    unit2,
    inv1,
    inv2,
    r1,
    g1,
    qkv_out,
    qkv_in,
    q_t,
    k_t,
    v_t,
    k_n,
    v_n,
    out_t,
    lse,
    mix_t,
    mixrows_t,
    upre,
    act,
    gp16,
    part_g2,
    in_g2,
    part_dn,
    in_dn,
    part_g1,
    in_g1,
    gm_out,
    gm_in,
    gq_t,
    gk_t,
    gv_t,
    gqkv_out,
    gqkv_in,
    gqkv,
    grads,
    core_in,
    a_in,
    b_in,
    a_sum,
    b_sum,
    a_last,
    b_last,
    vsum,
    tsum,
    sz_vec,
    sz_tp,
    v1,
    t1,
    s_y,
    s_yin,
    s_g,
    sg_c,
    sg_x,
    send_sems,
    recv_sems,
    local_sems,
):
    f, k, t = lax.axis_index("fsdp"), lax.axis_index("ctx"), lax.axis_index("tp")
    z, yh = f // 2, lax.rem(f, 2)
    yl, c = k // 2, lax.rem(k, 2)
    y = yh * 2 + yl
    head = t * 4 + k
    slope = slope_ref[0, 0]

    def at_zy(zz, yy, cc):
        return (zz * 2 + yy // 2, lax.rem(yy, 2) * 2 + cc, t)

    y_peers = [at_zy(z, around(y, d), c) for d in STEPS]
    z_peers = [at_zy(around(z, d), y, c) for d in STEPS]
    sibling = at_zy(z, y, 1 - c)
    opposite = at_zy(z, around(y, 2), c)
    ctx_peers = [(f, around(k, d), t) for d in STEPS]
    tp_peers = [(f, k, around(t, d)) for d in STEPS]
    group = [(dt, dk) for dt in range(4) for dk in range(4) if (dt, dk) != (0, 0)]

    def member(dt, dk):
        return (f, around(k, dk), around(t, dt))

    barrier = pltpu.get_barrier_semaphore()
    greeted = [member(dt, dk) for dt, dk in group] + y_peers + z_peers
    for partner in greeted:
        pl.semaphore_signal(barrier, inc=1, device_id=partner, device_id_type=MESH)
    pl.semaphore_wait(barrier, len(greeted))
    copies = Copies(send_sems, recv_sems)
    make = copies.make

    small_c = [make(small, near_c.at[d - 1], ctx_peers[d - 1]) for d in STEPS]
    far = [(dt, dk) for dt, dk in group if dt]
    small_x = [
        make(small.at[pl.ds(0, 8)], near_x.at[i], member(dt, dk)) for i, (dt, dk) in enumerate(far)
    ]

    upper, lower = pl.ds(0, 16), pl.ds(16, 16)

    def spread(src, cols):
        here = whole.at[z, y, c, :, cols]
        from_y = [make(src, here, peer) for peer in y_peers]
        from_z = [make(src, here, peer) for peer in z_peers]
        return from_y, from_z

    def relay(first, cols):
        from_y, from_z = first
        block = whole.at[z, :, c, :, cols]
        via = [[] for _ in STEPS]
        for d in STEPS:
            from_y[d - 1].wait_recv()
            piece = whole.at[z, around(y, 4 - d), c, upper, cols]
            for e in STEPS:
                via[e - 1].append(make(piece, piece, z_peers[e - 1]))
            from_z[d - 1].wait_recv()
            piece = whole.at[around(z, 4 - d), y, c, lower, cols]
            for e in STEPS:
                via[d - 1].append(make(piece, piece, y_peers[e - 1]))
        return via, [make(block, block, sibling)]

    def share(state, cols):
        via, core = state
        for e in STEPS:
            arrived(via[e - 1])
            block = whole.at[around(z, 4 - e), :, c, :, cols]
            core.append(make(block, block, sibling))
        return core

    local = [
        pltpu.make_async_copy(
            slab.at[:, pl.ds(2048, 768)], whole.at[z, y, c, :, QKV], local_sems.at[0]
        ),
        pltpu.make_async_copy(
            slab.at[:, pl.ds(0, 2048)], whole.at[z, y, c, :, slice(768, 2816)], local_sems.at[1]
        ),
        pltpu.make_async_copy(
            slab.at[:, pl.ds(2816, 256)],
            whole.at[z, y, c, :, pl.ds(pl.multiple_of(2816 + t * 256, 256), 256)],
            local_sems.at[2],
        ),
    ]
    for copy in local:
        copy.start()
    qkv_first = spread(slab.at[:, pl.ds(2048, 768)], QKV)
    out_cols = whole.at[z, y, c, :, pl.ds(pl.multiple_of(2816 + t * 256, 256), 256)]
    out_x = [make(slab.at[:, pl.ds(2816, 256)], out_cols, peer) for peer in tp_peers]

    r = hidden[...].astype(F32)
    centered = r - row_mean(r)
    rstd = lax.rsqrt(row_mean(centered * centered) + EPS)
    unit1[...] = centered * rstd
    inv1[...] = rstd
    gwide[t] = cot[...].astype(BF16)

    arrived(small_c)
    arrived(small_x)
    total = small[...] + near_c[0] + near_c[1] + near_c[2]
    norms = total[0:8]
    for i in range(12):
        norms = norms + near_x[i]
    tile_own[0:8] = norms
    tile_own[8:24] = total[8:24]
    small_z = [make(tile_own, tile_z.at[d - 1], z_peers[d - 1]) for d in STEPS]
    for copy in local:
        copy.wait()
    qkv_second = relay(qkv_first, QKV)
    arrived(small_z)
    pack_y[0] = tile_own[0:8]
    columns = tile_own[8:24]
    for d in STEPS:
        pack_y[d] = tile_z[d - 1, 0:8]
        columns = columns + tile_z[d - 1, 8:24]
    pack_y[4] = columns[0:8]
    pack_y[5] = columns[8:16]
    small_y = make(pack_y, pack_yin, opposite)
    small_y.wait_recv()
    for d in range(4):
        origin = around(z, 4 - d) * 2
        vec[:, pl.ds(pl.multiple_of((origin + yh) * 128, 128), 128)] = pack_y[d]
        vec[:, pl.ds(pl.multiple_of((origin + 1 - yh) * 128, 128), 128)] = pack_yin[d]
    first_rows = pack_y[4] + pack_yin[4]
    later_rows = pack_y[5] + pack_yin[5]
    rows = [first_rows[i : i + 1] for i in range(8)] + [later_rows[i : i + 1] for i in range(6)]
    for i in range(6):
        bias_q[:, i * 128 : (i + 1) * 128] = rows[i]
    for i in range(8):
        bias_u[:, i * 128 : (i + 1) * 128] = rows[6 + i]

    wide1[t] = (unit1[...] * vec[0:1] + vec[2:3]).astype(BF16)
    wide1_x = [make(wide1.at[t], wide1.at[t], peer) for peer in tp_peers]
    qkv_core = share(qkv_second, QKV)
    arrived(out_x)
    rest_first = spread(whole.at[z, y, c, :, REST], REST)
    arrived(qkv_core)
    arrived(wide1_x)
    cot_x = [make(gwide.at[t], gwide.at[t], peer) for peer in tp_peers]

    def project(n, carry):
        cols = pl.ds(pl.multiple_of(n * 256, 256), 256)
        out = dot(wide1[...].reshape(512, 1024), whole[:, :, :, :, cols].reshape(1024, 256))
        qkv_out[cols] = (out + bias_q[:, cols]).T.astype(BF16)
        return carry

    lax.fori_loop(0, 3, project, 0)

    def head_rows(j):
        return pl.ds(pl.multiple_of(j * 192, 64), 192)

    heads_c = [
        make(qkv_out.at[head_rows(around(k, d))], qkv_in.at[k], ctx_peers[d - 1]) for d in STEPS
    ]
    qkv_in[k] = qkv_out[head_rows(k)]
    rest_second = relay(rest_first, REST)
    arrived(heads_c)
    for i in range(4):
        span = slice(i * 512, (i + 1) * 512)
        q_t[:, span] = qkv_in[i, 0:64]
        keys = qkv_in[i, 64:128]
        values = qkv_in[i, 128:192]
        k_t[:, span] = keys
        v_t[:, span] = values
        k_n[span] = keys.T
        v_n[span] = values.T

    def scores(first, begin, width):
        at = pl.ds(first, BLOCK)
        s = dot(k_n[pl.ds(begin, width)], q_t[:, at])
        key = begin + lax.broadcasted_iota(jnp.int32, (width, BLOCK), 0)
        query = first + lax.broadcasted_iota(jnp.int32, (width, BLOCK), 1)
        s = s * 0.125 + slope * (key - first).astype(F32)
        return jnp.where((key <= query) & (key >= starts[:, at]), s, -jnp.inf)

    def attend(first, begin, width):
        at = pl.ds(first, BLOCK)
        s = scores(first, begin, width)
        highest = jnp.max(s, axis=0, keepdims=True)
        e = jnp.exp(s - highest)
        totals = jnp.sum(e, axis=0, keepdims=True)
        probs = (e * (1.0 / totals)).astype(BF16)
        out_t[:, at] = dot(v_t[:, pl.ds(begin, width)], probs).astype(BF16)
        lse[:, at] = highest + jnp.log(totals)

    def blocks(body):
        for b in range(4):
            body(b * BLOCK, 0, (b + 1) * BLOCK)

        def later(b, carry):
            begin = pl.multiple_of(b * BLOCK, BLOCK)
            body(pl.multiple_of(begin + 1024, BLOCK), begin, 1024 + BLOCK)
            return carry

        lax.fori_loop(0, 4, later, 0)

    blocks(attend)

    def own_lanes(kk, tt):
        return pl.ds(pl.multiple_of(kk * 512 + tt * 128, 128), 128)

    mine_rows = pl.ds(pl.multiple_of(head * 64, 64), 64)
    mix_g = [
        make(out_t.at[:, own_lanes(around(k, dk), around(t, dt))], mix_t.at[mine_rows], member(dt, dk))
        for dt, dk in group
    ]
    mix_t[mine_rows] = out_t[:, own_lanes(k, t)]
    rest_core = share(rest_second, REST)
    arrived(mix_g)
    local_rows = pl.ds(pl.multiple_of(k * 64, 64), 64)
    mixrows_c = [
        make(
            out_t.at[:, pl.ds(pl.multiple_of(around(k, d) * 512, 512), 512)],
            mixrows_t.at[local_rows],
            ctx_peers[d - 1],
        )
        for d in STEPS
    ]
    mixrows_t[local_rows] = out_t[:, pl.ds(pl.multiple_of(k * 512, 512), 512)]
    arrived(rest_core)

    for n in range(4):
        cols = slice(n * 256, (n + 1) * 256)
        out = dot(whole[n, :, :, :, OUT].reshape(256, 1024), mix_t[...])
        r1[:, cols] = hidden[:, cols].astype(F32) + out.T + vec[4:5, cols]
    r = r1[...]
    centered = r - row_mean(r)
    rstd = lax.rsqrt(row_mean(centered * centered) + EPS)
    unit2[...] = centered * rstd
    inv2[...] = rstd
    wide2[t] = (unit2[...] * vec[1:2] + vec[3:4]).astype(BF16)
    wide2_x = [make(wide2.at[t], wide2.at[t], peer) for peer in tp_peers]
    arrived(cot_x)

    def pull(n, carry):
        cols = pl.ds(pl.multiple_of(n * 256, 256), 256)
        wcols = pl.ds(pl.multiple_of(1792 + n * 256, 256), 256)
        upre[:, cols] = dot(
            gwide[...].reshape(512, 1024), whole[:, :, :, :, wcols].reshape(1024, 256)
        )
        return carry

    lax.fori_loop(0, 4, pull, 0)
    arrived(wide2_x)

    def feed(n, carry):
        cols = pl.ds(pl.multiple_of(n * 256, 256), 256)
        wcols = pl.ds(pl.multiple_of(768 + n * 256, 256), 256)
        pre = (
            dot(wide2[...].reshape(512, 1024), whole[:, :, :, :, wcols].reshape(1024, 256))
            + bias_u[:, cols]
        )
        curve = jnp.tanh(ROOT * (pre + CUBIC * pre * pre * pre))
        act[:, cols] = (0.5 * pre * (1.0 + curve)).astype(BF16)
        slant = 0.5 * (1.0 + curve) + 0.5 * pre * (1.0 - curve * curve) * ROOT * (
            1.0 + 3.0 * CUBIC * pre * pre
        )
        gpre = upre[:, cols] * slant
        gp16[:, cols] = gpre.astype(BF16)
        bias_u[:, cols] = jnp.sum(gpre, axis=0, keepdims=True)
        return carry

    lax.fori_loop(0, 4, feed, 0)

    def partial_rows(source, cols, part):
        def one(n, carry):
            width = cols.stop - cols.start
            out = dot(source[...], whole[n, :, :, :, cols].reshape(256, width), NT)
            part[:, :, pl.ds(pl.multiple_of(n * 256, 256), 256)] = out.astype(BF16).reshape(
                4, 128, 256
            )
            return carry

        lax.fori_loop(0, 4, one, 0)

    def send_rows(part, landing):
        return [
            make(part.at[around(t, d)], landing.at[d - 1], tp_peers[d - 1]) for d in STEPS
        ]

    def sum_rows(part, landing):
        total = part[t].astype(F32)
        for d in range(3):
            total = total + landing[d].astype(F32)
        return total

    partial_rows(gp16, UP, part_g2)
    g2_x = send_rows(part_g2, in_g2)

    def matrix_grad(left, right, chunk, offset, width):
        def one(m, carry):
            rows = left[:, :, pl.ds(pl.multiple_of(m * 256, 256), 256)].reshape(512, 256)
            out = dot(rows, right[...], TN)
            grads[chunk, m, :, :, :, pl.ds(offset, width)] = out.astype(BF16).reshape(
                4, 2, 32, width
            )
            return carry

        lax.fori_loop(0, 4, one, 0)

    def reduce_core(i):
        return make(grads.at[i, :, :, 1 - c], core_in.at[i], sibling)

    def reduce_first(i, core):
        core.wait_recv()

        def add(j, carry):
            zz, yy = j // 4, lax.rem(j, 4)
            total = grads[i, zz, yy, c].astype(F32) + core_in[i, zz, yy].astype(F32)
            core_in[i, zz, yy] = total.astype(BF16)
            return carry

        lax.fori_loop(0, 16, add, 0)
        a = [
            make(core_in.at[i, around(z, d), :, upper], a_in.at[i, d - 1], z_peers[d - 1])
            for d in STEPS
        ]
        b = [
            make(core_in.at[i, :, around(y, d), lower], b_in.at[i, d - 1], y_peers[d - 1])
            for d in STEPS
        ]
        return a, b

    def reduce_second(i, state):
        a, b = state
        arrived(a)

        def add_a(j, carry):
            total = core_in[i, z, j, 0:16].astype(F32)
            for d in range(3):
                total = total + a_in[i, d, j].astype(F32)
            a_sum[i, j] = total.astype(BF16)
            return carry

        lax.fori_loop(0, 4, add_a, 0)
        a = [make(a_sum.at[i, around(y, d)], a_last.at[i, d - 1], y_peers[d - 1]) for d in STEPS]
        arrived(b)

        def add_b(j, carry):
            total = core_in[i, j, y, 16:32].astype(F32)
            for d in range(3):
                total = total + b_in[i, d, j].astype(F32)
            b_sum[i, j] = total.astype(BF16)
            return carry

        lax.fori_loop(0, 4, add_b, 0)
        b = [make(b_sum.at[i, around(z, d)], b_last.at[i, d - 1], z_peers[d - 1]) for d in STEPS]
        return a, b

    def reduce_last(i, state):
        a, b = state
        cols = slice(i * WIDTH, (i + 1) * WIDTH)
        arrived(a)
        total = a_sum[i, y].astype(F32)
        for d in range(3):
            total = total + a_last[i, d].astype(F32)
        slab_out[0:16, cols] = total
        arrived(b)
        total = b_sum[i, z].astype(F32)
        for d in range(3):
            total = total + b_last[i, d].astype(F32)
        slab_out[16:32, cols] = total

    matrix_grad(wide2, gp16, 0, 0, 1024)
    up_state = reduce_core(0)
    partial_rows(act, DOWN, part_dn)

    def norm_back(total, unit, inv, gain):
        scaled = total * gain
        return inv * (scaled - row_mean(scaled) - unit * row_mean(scaled * unit))

    arrived(g2_x)
    dn_x = send_rows(part_dn, in_dn)
    total = sum_rows(part_g2, in_g2)
    vsum[1:2] = jnp.sum(total * unit2[...], axis=0, keepdims=True)
    vsum[3:4] = jnp.sum(total, axis=0, keepdims=True)
    vsum[5:6] = jnp.sum(cot[...], axis=0, keepdims=True)
    grad_mid = cot[...] + norm_back(total, unit2[...], inv2[...], vec[1:2])
    g1[...] = grad_mid
    vsum[4:5] = jnp.sum(grad_mid, axis=0, keepdims=True)
    gawide[t] = grad_mid.astype(BF16)
    for n in range(4):
        cols = slice(n * 256, (n + 1) * 256)
        wcols = slice(2816 + n * 256, 2816 + (n + 1) * 256)
        out = dot(gawide[t], whole[:, :, :, :, wcols].reshape(1024, 256))
        gm_out[cols] = out.T.astype(BF16)
    gm_g = [
        make(
            gm_out.at[
                pl.ds(pl.multiple_of((around(t, dt) * 4 + around(k, dk)) * 64, 64), 64)
            ],
            gm_in.at[:, own_lanes(k, t)],
            member(dt, dk),
        )
        for dt, dk in group
    ]
    gm_in[:, own_lanes(k, t)] = gm_out[mine_rows]
    up_state = reduce_first(0, up_state)
    matrix_grad(gwide, act, 1, 0, 1024)
    down_state = reduce_core(1)
    arrived(gm_g)
    ga_x = [make(gawide.at[t], gawide.at[t], peer) for peer in tp_peers]
    gk_t[...] = jnp.zeros_like(gk_t)
    gv_t[...] = jnp.zeros_like(gv_t)

    def attend_back(first, begin, width):
        at = pl.ds(first, BLOCK)
        window = pl.ds(begin, width)
        p = jnp.exp(scores(first, begin, width) - lse[:, at])
        grad = gm_in[:, at]
        gv_t[:, window] += dot(grad, p.astype(BF16), NT)
        dp = dot(v_n[window], grad)
        centre = jnp.sum(p * dp, axis=0, keepdims=True)
        ds = (p * (dp - centre) * 0.125).astype(BF16)
        gq_t[:, at] = dot(k_t[:, window], ds).astype(BF16)
        gk_t[:, window] += dot(q_t[:, at], ds, NT)

    for b in range(4):
        attend_back(b * BLOCK, 0, (b + 1) * BLOCK)
    up_state = reduce_second(0, up_state)
    down_state = reduce_first(1, down_state)

    def later_back(b, carry):
        begin = pl.multiple_of(b * BLOCK, BLOCK)
        attend_back(pl.multiple_of(begin + 1024, BLOCK), begin, 1024 + BLOCK)
        return carry

    lax.fori_loop(0, 4, later_back, 0)
    for j in range(4):
        span = slice(j * 512, (j + 1) * 512)
        gqkv_out[j, 0:64] = gq_t[:, span]
        gqkv_out[j, 64:128] = gk_t[:, span].astype(BF16)
        gqkv_out[j, 128:192] = gv_t[:, span].astype(BF16)
    back_c = [
        make(gqkv_out.at[around(k, d)], gqkv_in.at[k], ctx_peers[d - 1]) for d in STEPS
    ]
    gqkv_in[k] = gqkv_out[k]
    arrived(ga_x)
    arrived(mixrows_c)
    gp16[:, 0:256] = mixrows_t[...].T
    matrix_grad(gawide, gp16.at[:, pl.ds(0, 256)], 2, 768, 256)
    reduce_last(0, up_state)
    down_state = reduce_second(1, down_state)
    arrived(dn_x)
    r2_out[...] = r1[...] + sum_rows(part_dn, in_dn) + vec[5:6]
    arrived(back_c)
    gqkv[...] = gqkv_in[...].reshape(768, 512).T
    partial_rows(gqkv, QKV, part_g1)
    g1_x = send_rows(part_g1, in_g1)
    sums = jnp.sum(gqkv[...].astype(F32), axis=0, keepdims=True)
    for i in range(6):
        tsum[i : i + 1] = sums[:, i * 128 : (i + 1) * 128]
    for i in range(8):
        tsum[6 + i : 7 + i] = bias_u[:, i * 128 : (i + 1) * 128]
    tsum[14:16] = jnp.zeros((2, 128), F32)
    matrix_grad(wide1, gqkv, 2, 0, 768)
    qkv_state = reduce_core(2)
    reduce_last(1, down_state)

    arrived(g1_x)
    qkv_state = reduce_first(2, qkv_state)
    total = sum_rows(part_g1, in_g1)
    vsum[0:1] = jnp.sum(total * unit1[...], axis=0, keepdims=True)
    vsum[2:3] = jnp.sum(total, axis=0, keepdims=True)
    vsum[6:8] = jnp.zeros((2, 1024), F32)
    sum_z = [
        make(
            vsum.at[:, pl.ds(pl.multiple_of(around(z, d) * 256, 256), 256)],
            sz_vec.at[d - 1],
            z_peers[d - 1],
        )
        for d in STEPS
    ] + [make(tsum, sz_tp.at[d - 1], z_peers[d - 1]) for d in STEPS]
    g0_out[...] = g1[...] + norm_back(total, unit1[...], inv1[...], vec[0:1])
    arrived(sum_z)
    v1[...] = (
        vsum[:, pl.ds(pl.multiple_of(z * 256, 256), 256)] + sz_vec[0] + sz_vec[1] + sz_vec[2]
    )
    t1[...] = tsum[...] + sz_tp[0] + sz_tp[1] + sz_tp[2]
    s_y[0:8] = v1[:, pl.ds(pl.multiple_of((1 - yh) * 128, 128), 128)]
    s_y[8:24] = t1[...]
    sum_y = make(s_y, s_yin, opposite)
    qkv_state = reduce_second(2, qkv_state)
    sum_y.wait_recv()
    s_g[0:8] = v1[:, pl.ds(pl.multiple_of(yh * 128, 128), 128)] + s_yin[0:8]
    s_g[8:24] = t1[...] + s_yin[8:24]
    sum_c = [make(s_g, sg_c.at[d - 1], ctx_peers[d - 1]) for d in STEPS]
    sum_x = [
        make(s_g.at[pl.ds(0, 8)], sg_x.at[i], member(dt, dk)) for i, (dt, dk) in enumerate(far)
    ]
    reduce_last(2, qkv_state)
    arrived(sum_c)
    arrived(sum_x)
    total = s_g[...] + sg_c[0] + sg_c[1] + sg_c[2]
    norms = total[0:8]
    for i in range(12):
        norms = norms + sg_x[i]
    small_out[0:8] = norms
    small_out[8:24] = total[8:24]
    copies.finish()


COUNT = 220


def run_layer(slab, small, hidden, cot, starts, slope):
    vmem = pltpu.VMEM
    scratch = [
        vmem((4, 4, 2, 32, WIDE), BF16),
        vmem((3, 24, 128), F32),
        vmem((12, 8, 128), F32),
        vmem((24, 128), F32),
        vmem((3, 24, 128), F32),
        vmem((6, 8, 128), F32),
        vmem((6, 8, 128), F32),
        vmem((8, 1024), F32),
        vmem((1, 768), F32),
        vmem((1, 1024), F32),
        vmem((4, 128, 1024), BF16),
        vmem((4, 128, 1024), BF16),
        vmem((4, 128, 1024), BF16),
        vmem((4, 128, 1024), BF16),
        vmem((128, 1024), F32),
        vmem((128, 1024), F32),
        vmem((128, 1), F32),
        vmem((128, 1), F32),
        vmem((128, 1024), F32),
        vmem((128, 1024), F32),
        vmem((768, 512), BF16),
        vmem((4, 192, 512), BF16),
        vmem((64, 2048), BF16),
        vmem((64, 2048), BF16),
        vmem((64, 2048), BF16),
        vmem((2048, 64), BF16),
        vmem((2048, 64), BF16),
        vmem((64, 2048), BF16),
        vmem((1, 2048), F32),
        vmem((1024, 128), BF16),
        vmem((256, 512), BF16),
        vmem((512, 1024), F32),
        vmem((512, 1024), BF16),
        vmem((512, 1024), BF16),
        vmem((4, 128, 1024), BF16),
        vmem((3, 128, 1024), BF16),
        vmem((4, 128, 1024), BF16),
        vmem((3, 128, 1024), BF16),
        vmem((4, 128, 1024), BF16),
        vmem((3, 128, 1024), BF16),
        vmem((1024, 128), BF16),
        vmem((64, 2048), BF16),
        vmem((64, 2048), BF16),
        vmem((64, 2048), F32),
        vmem((64, 2048), F32),
        vmem((4, 192, 512), BF16),
        vmem((4, 192, 512), BF16),
        vmem((512, 768), BF16),
        vmem((CHUNKS, 4, 4, 2, 32, WIDTH), BF16),
        vmem((CHUNKS, 4, 4, 32, WIDTH), BF16),
        vmem((CHUNKS, 3, 4, 16, WIDTH), BF16),
        vmem((CHUNKS, 3, 4, 16, WIDTH), BF16),
        vmem((CHUNKS, 4, 16, WIDTH), BF16),
        vmem((CHUNKS, 4, 16, WIDTH), BF16),
        vmem((CHUNKS, 3, 16, WIDTH), BF16),
        vmem((CHUNKS, 3, 16, WIDTH), BF16),
        vmem((8, 1024), F32),
        vmem((16, 128), F32),
        vmem((3, 8, 256), F32),
        vmem((3, 16, 128), F32),
        vmem((8, 256), F32),
        vmem((16, 128), F32),
        vmem((24, 128), F32),
        vmem((24, 128), F32),
        vmem((24, 128), F32),
        vmem((3, 24, 128), F32),
        vmem((12, 8, 128), F32),
        pltpu.SemaphoreType.DMA((COUNT,)),
        pltpu.SemaphoreType.DMA((COUNT,)),
        pltpu.SemaphoreType.DMA((3,)),
    ]
    whole_vmem = pl.BlockSpec(memory_space=pltpu.VMEM)
    return pl.pallas_call(
        layer_kernel,
        out_shape=(
            jax.ShapeDtypeStruct((128, 1024), F32),
            jax.ShapeDtypeStruct((128, 1024), F32),
            jax.ShapeDtypeStruct((32, SLAB), F32),
            jax.ShapeDtypeStruct((24, 128), F32),
        ),
        in_specs=[whole_vmem] * 5 + [pl.BlockSpec(memory_space=pltpu.SMEM)],
        out_specs=(whole_vmem,) * 4,
        scratch_shapes=scratch,
        compiler_params=pltpu.CompilerParams(
            collective_id=0, has_side_effects=True, vmem_limit_bytes=60 << 20
        ),
        name="layer",
    )(slab, small, hidden, cot, starts, slope)


def on_device(
    hidden_in,
    segment_ids,
    norm_gain,
    norm_bias,
    w_qkv,
    qv_bias,
    w_out,
    out_bias,
    w_up,
    up_bias,
    w_down,
    cotangent,
):
    f, k, t = lax.axis_index("fsdp"), lax.axis_index("ctx"), lax.axis_index("tp")
    slope = jnp.exp2(-8.0 * (t * 4 + k + 1).astype(F32) / H).reshape(1, 1)
    segments = segment_ids[0]
    starts = jnp.zeros((2048,), jnp.int32)
    for value in range(1, 4):
        starts = jnp.where(
            segments >= value, jnp.sum((segments < value).astype(jnp.int32)), starts
        )
    starts = starts.reshape(1, 2048)

    qkv_cols = w_qkv[0].reshape(3, 32, 4, 64).transpose(1, 2, 0, 3).reshape(32, 768)
    slab = jnp.concatenate([w_up[0], w_down[0], qkv_cols, w_out[0]], axis=1)

    norms = jnp.concatenate([norm_gain[0], norm_bias[0], out_bias[0], jnp.zeros((2, 8), F32)])
    lane = jnp.arange(128, dtype=jnp.int32)
    norms = jnp.where(lane[None] // 8 == k * 4 + t, jnp.tile(norms, (1, 16)), 0.0)
    qv = qv_bias[0].astype(F32)
    qv = jnp.where(lane[None, None, :64] // 2 == f * 4 + k, jnp.tile(qv, (1, 1, 32)), 0.0)
    qkv_bias = jnp.stack([qv[0], jnp.zeros_like(qv[0]), qv[1]], axis=1).reshape(6, 128)
    lane = jnp.arange(256, dtype=jnp.int32)
    up = jnp.where(
        lane[None] // 8 == f * 4 + k, jnp.tile(up_bias[0].astype(F32), (1, 32)), 0.0
    ).reshape(8, 128)
    small = jnp.concatenate([norms, qkv_bias, up, jnp.zeros((2, 128), F32)])

    hidden_out, grad_input, out, sums = run_layer(
        slab, small, hidden_in, cotangent, starts, slope
    )

    norm_sums = lax.dynamic_slice_in_dim(sums[0:6], (k * 4 + t) * 8, 8, 1)
    qkv_sums = sums[8:14].reshape(4, 3, 64)
    qv_sums = lax.dynamic_slice_in_dim(
        jnp.stack([qkv_sums[:, 0], qkv_sums[:, 2]]), (f * 4 + k) * 2, 2, 2
    )
    up_sums = lax.dynamic_slice_in_dim(sums[14:22].reshape(4, 256), (f * 4 + k) * 8, 8, 1)
    return (
        hidden_out,
        grad_input,
        norm_sums[0:2].reshape(1, 2, 8),
        norm_sums[2:4].reshape(1, 2, 8),
        out[:, 2048:2816].reshape(32, 4, 3, 64).transpose(2, 0, 1, 3).reshape(1, 3, 32, 256),
        qv_sums.reshape(1, 2, 4, 2),
        out[:, 2816:3072].reshape(1, 32, 256),
        norm_sums[4:6].reshape(1, 2, 8),
        out[:, 0:1024].reshape(1, 32, 1024),
        up_sums.reshape(1, 4, 8),
        out[:, 1024:2048].reshape(1, 32, 1024),
    )


def solution(mesh):
    return jax.shard_map(
        on_device,
        mesh=mesh,
        in_specs=(
            P(("fsdp", "ctx", "tp"), None),
            P("fsdp", None),
            P(None, None, ("fsdp", "ctx", "tp")),
            P(None, None, ("fsdp", "ctx", "tp")),
            P(None, None, ("fsdp", "ctx"), "tp"),
            P(None, None, "tp", ("fsdp", "ctx")),
            P(None, ("fsdp", "ctx"), "tp"),
            P(None, None, ("fsdp", "ctx", "tp")),
            P(None, ("fsdp", "ctx"), "tp"),
            P(None, "tp", ("fsdp", "ctx")),
            P(None, ("fsdp", "ctx"), "tp"),
            P(("fsdp", "ctx", "tp"), None),
        ),
        out_specs=(
            P(("fsdp", "ctx", "tp"), None),
            P(("fsdp", "ctx", "tp"), None),
            P(None, None, ("fsdp", "ctx", "tp")),
            P(None, None, ("fsdp", "ctx", "tp")),
            P(None, None, ("fsdp", "ctx"), "tp"),
            P(None, None, "tp", ("fsdp", "ctx")),
            P(None, ("fsdp", "ctx"), "tp"),
            P(None, None, ("fsdp", "ctx", "tp")),
            P(None, ("fsdp", "ctx"), "tp"),
            P(None, "tp", ("fsdp", "ctx")),
            P(None, ("fsdp", "ctx"), "tp"),
        ),
        check_vma=False,
    )
```

```python
import jax
import jax.numpy as jnp
from jax import lax
from jax.experimental import pallas as pl
from jax.experimental.pallas import tpu as pltpu
from jax.sharding import PartitionSpec as P

H = 16
HD = 64
EPS = 1e-05
ROOT = 0.7978845608028654
CUBIC = 0.044715
NN = (((1,), (0,)), ((), ()))
NT = (((1,), (1,)), ((), ()))
TN = (((0,), (0,)), ((), ()))
MESH = pl.DeviceIdType.MESH
F32 = jnp.float32
BF16 = jnp.bfloat16
STEPS = (1, 2, 3)

QKV = slice(0, 768)
UP = slice(768, 1792)
DOWN = slice(1792, 2816)
OUT = slice(2816, 3840)
MLP = slice(768, 2816)
WIDE = 3840
SLAB = 3072
CHUNKS = ((0, 1024), (1024, 1024), (2816, 256), (2048, 768))
BLOCK = 256


def around(index, step):
    return lax.rem(index + step, 4)


def dot(a, b, dims=NN):
    return lax.dot_general(a, b, dims, preferred_element_type=F32)


class Copies:
    def __init__(self, send_sems, recv_sems):
        self.send_sems, self.recv_sems, self.used, self.all = send_sems, recv_sems, 0, []

    def make(self, src, dst, target):
        index = self.used
        self.used += 1
        assert index < COUNT
        copy = pltpu.make_async_remote_copy(
            src_ref=src,
            dst_ref=dst,
            send_sem=self.send_sems.at[index],
            recv_sem=self.recv_sems.at[index],
            device_id=target,
            device_id_type=MESH,
        )
        copy.start()
        self.all.append(copy)
        return copy

    def finish(self):
        for copy in self.all:
            copy.wait_send()


def step(*works):
    for work in works:
        next(work, None)


def arrived(copies):
    for copy in copies:
        copy.wait_recv()


def row_mean(x):
    return jnp.mean(x, axis=1, keepdims=True)


def layer_kernel(
    w_up,
    w_down,
    w_qkv,
    w_out,
    gain_in,
    shift_in,
    obias_in,
    qv_in,
    ub_in,
    hidden,
    cot,
    segments,
    r2_out,
    g0_out,
    slab_out,
    small_out,
    whole,
    small,
    starts,
    near_c,
    near_x,
    tile_own,
    tile_z,
    pack_y,
    pack_yin,
    vec,
    bias_q,
    bias_u,
    wide1,
    gwide,
    wide2,
    gawide,
    unit1,
    unit2,
    inv1,
    inv2,
    r1,
    g1,
    qkv_out,
    qkv_in,
    q_t,
    k_t,
    v_t,
    k_n,
    v_n,
    out_t,
    lse,
    mix_t,
    mixrows_t,
    upre,
    act,
    gp16,
    part_g2,
    via_g2,
    in_g2,
    part_dn,
    via_dn,
    in_dn,
    part_g1,
    via_g1,
    in_g1,
    gm_out,
    gm_in,
    gq_t,
    gk_t,
    gv_t,
    gqkv_out,
    gqkv_in,
    gqkv,
    grads,
    core_in,
    a_via,
    b_via,
    a_in,
    b_in,
    a_sum,
    b_sum,
    a_lastvia,
    b_lastvia,
    a_last,
    b_last,
    vsum,
    tsum,
    sz_vec,
    sz_tp,
    v1,
    t1,
    s_y,
    s_yin,
    s_g,
    sg_c,
    sg_x,
    send_sems,
    recv_sems,
):
    f, k, t = lax.axis_index("fsdp"), lax.axis_index("ctx"), lax.axis_index("tp")
    z, yh = f // 2, lax.rem(f, 2)
    yl, c = k // 2, lax.rem(k, 2)
    y = yh * 2 + yl
    head = t * 4 + k
    place = f * 4 + k
    slope = jnp.exp2(jnp.full((1, BLOCK), -8.0 / H, F32) * (head + 1).astype(F32))

    def at_zy(zz, yy, cc):
        return (zz * 2 + yy // 2, lax.rem(yy, 2) * 2 + cc, t)

    y_peers = [at_zy(z, around(y, d), c) for d in STEPS]
    z_peers = [at_zy(around(z, d), y, c) for d in STEPS]
    sibling = at_zy(z, y, 1 - c)
    opposite = at_zy(z, around(y, 2), c)
    ctx_peers = [(f, around(k, d), t) for d in STEPS]
    tp_peers = [(f, k, around(t, d)) for d in STEPS]
    group = [(dt, dk) for dt in range(4) for dk in range(4) if (dt, dk) != (0, 0)]

    def member(dt, dk):
        return (f, around(k, dk), around(t, dt))

    barrier = pltpu.get_barrier_semaphore()
    greeted = [member(dt, dk) for dt, dk in group] + y_peers + z_peers
    for partner in greeted:
        pl.semaphore_signal(barrier, inc=1, device_id=partner, device_id_type=MESH)
    pl.semaphore_wait(barrier, len(greeted))
    copies = Copies(send_sems, recv_sems)
    make = copies.make

    def lanes(count, period, index):
        row = lax.broadcasted_iota(jnp.int32, (count, 128), 0)
        lane = lax.broadcasted_iota(jnp.int32, (count, 128), 1)
        return ((lane % count == row) & ((lane % period) // count == index)).astype(F32)

    def scatter(values, hot):
        return lax.dot_general(
            values.astype(F32), hot, NN, precision=lax.Precision.HIGHEST, preferred_element_type=F32
        )

    small[...] = jnp.zeros_like(small)
    own = lanes(8, 128, k * 4 + t)
    small[0:2] = scatter(gain_in[0], own)
    small[2:4] = scatter(shift_in[0], own)
    small[4:6] = scatter(obias_in[0], own)
    pair = lanes(2, 64, place)
    left = lax.broadcasted_iota(jnp.int32, (4, 128), 1) < 64
    q_row, v_row = scatter(qv_in[0, 0], pair), scatter(qv_in[0, 1], pair)
    q_left, q_right = jnp.where(left, q_row, 0.0), jnp.where(left, 0.0, q_row)
    v_left, v_right = jnp.where(left, v_row, 0.0), jnp.where(left, 0.0, v_row)
    small[8:9] = q_left[0:1]
    small[9:10] = v_left[0:1] + q_right[1:2]
    small[10:11] = v_right[1:2]
    small[11:12] = q_left[2:3]
    small[12:13] = v_left[2:3] + q_right[3:4]
    small[13:14] = v_right[3:4]
    up_row = scatter(ub_in[0], lanes(8, 128, lax.rem(place, 16)))
    even = (place < 16).astype(F32)
    for i in range(4):
        small[14 + 2 * i : 15 + 2 * i] = up_row[i : i + 1] * even
        small[15 + 2 * i : 16 + 2 * i] = up_row[i : i + 1] * (1.0 - even)
    small_c = [make(small, near_c.at[d - 1], ctx_peers[d - 1]) for d in STEPS]
    far = [(dt, dk) for dt, dk in group if dt]
    small_x = [
        make(small.at[pl.ds(0, 8)], near_x.at[i], member(dt, dk)) for i, (dt, dk) in enumerate(far)
    ]

    upper, lower = pl.ds(0, 16), pl.ds(16, 16)
    low, high = pl.ds(0, 2), pl.ds(2, 2)

    def ring(part, me, peers):
        plus, minus = peers[0], peers[2]
        u, v = part(me)
        plus_u, minus_v = make(u, u, plus), make(v, v, minus)
        plus_v, minus_u = make(v, v, plus), make(u, u, minus)

        def forward():
            plus_u.wait_recv()
            u = part(around(me, 3))[0]
            next_u = make(u, u, plus)
            minus_v.wait_recv()
            v = part(around(me, 1))[1]
            return [plus_v, minus_u, next_u, make(v, v, minus)]

        return forward

    def ring_rows(buffer):
        return ring(
            lambda o: (buffer.at[o, :, pl.ds(0, 512)], buffer.at[o, :, pl.ds(512, 512)]),
            t,
            tp_peers,
        )

    def ring_sum(part, via, land, me, peers, filled=None):
        plus, minus = peers[0], peers[2]
        one, two, three = around(me, 1), around(me, 2), around(me, 3)
        if filled:
            filled(0)
        via_u = make(part(two)[0], via[0], plus)
        near_u = make(part(three)[0], land[1][0], minus)
        if filled:
            filled(1)
        via_v = make(part(two)[1], via[1], minus)
        near_v = make(part(one)[1], land[0][1], plus)
        yield
        via_u.wait_recv()
        via[0][...] = (via[0][...].astype(F32) + part(one)[0][...].astype(F32)).astype(BF16)
        next_u = make(via[0], land[0][0], plus)
        via_v.wait_recv()
        via[1][...] = (via[1][...].astype(F32) + part(three)[1][...].astype(F32)).astype(BF16)
        next_v = make(via[1], land[1][1], minus)
        yield
        arrived([near_u, near_v, next_u, next_v])

    def ring_sum_rows(part, via, land, filled=None):
        ends = pl.ds(0, 512), pl.ds(512, 512)
        return ring_sum(
            lambda o: tuple(part.at[o, :, end] for end in ends),
            (via.at[0], via.at[1]),
            tuple(tuple(land.at[i, :, end] for end in ends) for i in range(2)),
            t,
            tp_peers,
            filled,
        )

    def gather(cols):
        middle = (cols.start + cols.stop) // 2
        ends = slice(cols.start, middle), slice(middle, cols.stop)
        a = ring(lambda o: tuple(whole.at[z, o, c, upper, end] for end in ends), y, y_peers)
        b = ring(lambda o: tuple(whole.at[o, y, c, lower, end] for end in ends), z, z_peers)
        yield
        a, b = a(), b()
        yield
        arrived(a)
        a = ring(lambda o: tuple(whole.at[o, yy, c, upper, cols] for yy in (low, high)), z, z_peers)
        arrived(b)
        b = ring(lambda o: tuple(whole.at[zz, o, c, lower, cols] for zz in (low, high)), y, y_peers)

        def both(d):
            for block in (
                whole.at[around(z, d), :, c, upper, cols],
                whole.at[:, around(y, d), c, lower, cols],
            ):
                core.append(make(block, block, sibling))

        core = []
        both(0)
        yield
        a, b = a(), b()
        yield
        arrived(a + b)
        for d in STEPS:
            both(d)
        yield
        arrived(core)

    for j in range(4):
        for i in range(3):
            col = j * 192 + i * 64
            whole[z, y, c, :, col : col + 64] = w_qkv[0, i, :, j * 64 : j * 64 + 64]
    gather_qkv = gather(QKV)
    step(gather_qkv)
    own_out = pl.ds(pl.multiple_of(2816 + t * 256, 256), 256)
    whole[z, y, c, :, own_out] = w_out[0]
    out_cols = whole.at[z, y, c, :, own_out]
    out_x = [make(out_cols, out_cols, peer) for peer in tp_peers]
    whole[z, y, c, :, 768:1792] = w_up[0]
    whole[z, y, c, :, 1792:2816] = w_down[0]

    r = hidden[...].astype(F32)
    centered = r - row_mean(r)
    rstd = lax.rsqrt(row_mean(centered * centered) + EPS)
    unit1[...] = centered * rstd
    inv1[...] = rstd

    arrived(small_c)
    arrived(small_x)
    total = small[...] + near_c[0] + near_c[1] + near_c[2]
    norms = total[0:8]
    for i in range(12):
        norms = norms + near_x[i]
    tile_own[0:8] = norms
    tile_own[8:24] = total[8:24]
    small_z = [make(tile_own, tile_z.at[d - 1], z_peers[d - 1]) for d in STEPS]
    step(gather_qkv)
    arrived(small_z)
    pack_y[0] = tile_own[0:8]
    columns = tile_own[8:24]
    for d in STEPS:
        pack_y[d] = tile_z[d - 1, 0:8]
        columns = columns + tile_z[d - 1, 8:24]
    pack_y[4] = columns[0:8]
    pack_y[5] = columns[8:16]
    small_y = make(pack_y, pack_yin, opposite)
    step(gather_qkv)
    small_y.wait_recv()
    for d in range(4):
        origin = around(z, 4 - d) * 2
        vec[:, pl.ds(pl.multiple_of((origin + yh) * 128, 128), 128)] = pack_y[d]
        vec[:, pl.ds(pl.multiple_of((origin + 1 - yh) * 128, 128), 128)] = pack_yin[d]
    first_rows = pack_y[4] + pack_yin[4]
    later_rows = pack_y[5] + pack_yin[5]
    rows = [first_rows[i : i + 1] for i in range(8)] + [later_rows[i : i + 1] for i in range(6)]
    for i in range(6):
        bias_q[:, i * 128 : (i + 1) * 128] = rows[i]
    for i in range(8):
        bias_u[:, i * 128 : (i + 1) * 128] = rows[6 + i]

    wide1[t] = (unit1[...] * vec[0:1] + vec[2:3]).astype(BF16)
    wide1_x = ring_rows(wide1)
    step(gather_qkv)
    arrived(out_x)
    gather_out = gather(OUT)
    step(gather_out)
    wide1_x = wide1_x()
    gwide[t] = cot[...].astype(BF16)
    ids = segments[...]
    first = jnp.zeros((1, 2048), F32)
    for value in range(1, 4):
        count = jnp.sum((ids < value).astype(F32), axis=1, keepdims=True)
        first = jnp.where(ids >= value, count, first)
    starts[...] = first
    step(gather_qkv)
    step(gather_out)
    step(gather_qkv)
    arrived(wide1_x)
    gwide_x = ring_rows(gwide)

    def project(n, carry):
        cols = pl.ds(pl.multiple_of(n * 256, 256), 256)
        out = dot(wide1[...].reshape(512, 1024), whole[:, :, :, :, cols].reshape(1024, 256))
        qkv_out[cols] = (out + bias_q[:, cols]).T.astype(BF16)
        return carry

    lax.fori_loop(0, 3, project, 0)

    def head_rows(j):
        return pl.ds(pl.multiple_of(j * 192, 64), 192)

    heads_c = [
        make(qkv_out.at[head_rows(around(k, d))], qkv_in.at[k], ctx_peers[d - 1]) for d in STEPS
    ]
    qkv_in[k] = qkv_out[head_rows(k)]
    step(gather_out)
    gather_mlp = gather(MLP)
    step(gather_mlp)
    gwide_x = gwide_x()
    step(gather_out)
    arrived(heads_c)
    for i in range(4):
        span = slice(i * 512, (i + 1) * 512)
        q_t[:, span] = qkv_in[i, 0:64]
        keys = qkv_in[i, 64:128]
        values = qkv_in[i, 128:192]
        k_t[:, span] = keys
        v_t[:, span] = values
        k_n[span] = keys.T
        v_n[span] = values.T

    def scores(first, begin, width):
        at = pl.ds(first, BLOCK)
        s = dot(k_n[pl.ds(begin, width)], q_t[:, at])
        key = begin + lax.broadcasted_iota(jnp.int32, (width, BLOCK), 0)
        query = first + lax.broadcasted_iota(jnp.int32, (width, BLOCK), 1)
        s = s * 0.125 + slope * (key - first).astype(F32)
        return jnp.where((key <= query) & (key.astype(F32) >= starts[:, at]), s, -jnp.inf)

    def attend(first, begin, width):
        at = pl.ds(first, BLOCK)
        s = scores(first, begin, width)
        highest = jnp.max(s, axis=0, keepdims=True)
        e = jnp.exp(s - highest)
        totals = jnp.sum(e, axis=0, keepdims=True)
        probs = (e * (1.0 / totals)).astype(BF16)
        out_t[:, at] = dot(v_t[:, pl.ds(begin, width)], probs).astype(BF16)
        lse[:, at] = highest + jnp.log(totals)

    def blocks(body, *between):
        def later(b, carry):
            begin = pl.multiple_of(b * BLOCK, BLOCK)
            body(pl.multiple_of(begin + 1024, BLOCK), begin, 1024 + BLOCK)
            return carry

        for b in range(4):
            body(b * BLOCK, 0, (b + 1) * BLOCK)
            if b == 1:
                between[0]()
        between[1]()
        lax.fori_loop(0, 2, later, 0)
        between[2]()
        lax.fori_loop(2, 4, later, 0)
        between[3]()

    blocks(
        attend,
        lambda: step(gather_out, gather_mlp),
        lambda: step(gather_mlp),
        lambda: step(gather_mlp),
        lambda: None,
    )

    def own_lanes(kk, tt):
        return pl.ds(pl.multiple_of(kk * 512 + tt * 128, 128), 128)

    mine_rows = pl.ds(pl.multiple_of(head * 64, 64), 64)
    mix_g = [
        make(out_t.at[:, own_lanes(around(k, dk), around(t, dt))], mix_t.at[mine_rows], member(dt, dk))
        for dt, dk in group
    ]
    mix_t[mine_rows] = out_t[:, own_lanes(k, t)]
    step(gather_out, gather_mlp)
    arrived(mix_g)
    local_rows = pl.ds(pl.multiple_of(k * 64, 64), 64)
    mixrows_c = [
        make(
            out_t.at[:, pl.ds(pl.multiple_of(around(k, d) * 512, 512), 512)],
            mixrows_t.at[local_rows],
            ctx_peers[d - 1],
        )
        for d in STEPS
    ]
    mixrows_t[local_rows] = out_t[:, pl.ds(pl.multiple_of(k * 512, 512), 512)]

    for n in range(4):
        cols = slice(n * 256, (n + 1) * 256)
        out = dot(whole[n, :, :, :, OUT].reshape(256, 1024), mix_t[...])
        r1[:, cols] = hidden[:, cols].astype(F32) + out.T + vec[4:5, cols]
    r = r1[...]
    centered = r - row_mean(r)
    rstd = lax.rsqrt(row_mean(centered * centered) + EPS)
    unit2[...] = centered * rstd
    inv2[...] = rstd
    wide2[t] = (unit2[...] * vec[1:2] + vec[3:4]).astype(BF16)
    wide2_x = ring_rows(wide2)
    step(gather_mlp)
    arrived(gwide_x)

    def pull(n, carry):
        cols = pl.ds(pl.multiple_of(n * 256, 256), 256)
        wcols = pl.ds(pl.multiple_of(1792 + n * 256, 256), 256)
        upre[:, cols] = dot(
            gwide[...].reshape(512, 1024), whole[:, :, :, :, wcols].reshape(1024, 256)
        )
        return carry

    lax.fori_loop(0, 2, pull, 0)
    wide2_x = wide2_x()
    lax.fori_loop(2, 4, pull, 0)
    arrived(wide2_x)

    def feed(n, carry):
        cols = pl.ds(pl.multiple_of(n * 256, 256), 256)
        wcols = pl.ds(pl.multiple_of(768 + n * 256, 256), 256)
        pre = (
            dot(wide2[...].reshape(512, 1024), whole[:, :, :, :, wcols].reshape(1024, 256))
            + bias_u[:, cols]
        )
        curve = jnp.tanh(ROOT * (pre + CUBIC * pre * pre * pre))
        act[:, cols] = (0.5 * pre * (1.0 + curve)).astype(BF16)
        slant = 0.5 * (1.0 + curve) + 0.5 * pre * (1.0 - curve * curve) * ROOT * (
            1.0 + 3.0 * CUBIC * pre * pre
        )
        gpre = upre[:, cols] * slant
        gp16[:, cols] = gpre.astype(BF16)
        bias_u[:, cols] = jnp.sum(gpre, axis=0, keepdims=True)
        return carry

    lax.fori_loop(0, 4, feed, 0)

    def partial_rows(source, cols, part):
        def one(n, carry):
            width = cols.stop - cols.start
            out = dot(source[...], whole[n, :, :, :, cols].reshape(256, width), NT)
            part[:, :, pl.ds(pl.multiple_of(n * 256, 256), 256)] = out.astype(BF16).reshape(
                4, 128, 256
            )
            return carry

        return lambda half: lax.fori_loop(2 * half, 2 * half + 2, one, 0)

    def sum_rows(part, landing):
        return part[t].astype(F32) + landing[0].astype(F32) + landing[1].astype(F32)

    sum_g2 = ring_sum_rows(part_g2, via_g2, in_g2, partial_rows(gp16, UP, part_g2))
    step(sum_g2)

    def matrix_grad(left, right, chunk):
        width = CHUNKS[chunk][1]

        def one(m, carry):
            rows = left[:, :, pl.ds(pl.multiple_of(m * 256, 256), 256)].reshape(512, 256)
            out = dot(rows, right[...], TN)
            grads[chunk][m] = out.astype(BF16).reshape(4, 2, 32, width)
            return carry

        lax.fori_loop(0, 4, one, 0)

    def reduce(i):
        offset, width = CHUNKS[i]
        both = core_in[i]
        core = make(grads[i].at[:, :, 1 - c], both, sibling)
        yield
        core.wait_recv()

        def add(j, carry):
            zz, yy = j // 4, lax.rem(j, 4)
            total = grads[i][zz, yy, c].astype(F32) + both[zz, yy].astype(F32)
            both[zz, yy] = total.astype(BF16)
            return carry

        lax.fori_loop(0, 16, add, 0)
        yield
        a = ring_sum(
            lambda o: (both.at[o, low, upper], both.at[o, high, upper]),
            (a_via[i].at[low], a_via[i].at[high]),
            tuple((a_in[i].at[d, low], a_in[i].at[d, high]) for d in range(2)),
            z,
            z_peers,
        )
        b = ring_sum(
            lambda o: (both.at[low, o, lower], both.at[high, o, lower]),
            (b_via[i].at[low], b_via[i].at[high]),
            tuple((b_in[i].at[d, low], b_in[i].at[d, high]) for d in range(2)),
            y,
            y_peers,
        )
        step(a, b)
        yield
        step(a, b)
        yield
        step(a)
        for j in range(4):
            total = both[z, j, 0:16].astype(F32)
            for d in range(2):
                total = total + a_in[i][d, j].astype(F32)
            a_sum[i][j] = total.astype(BF16)
        ends = pl.ds(0, width // 2), pl.ds(width // 2, width // 2)
        a = ring_sum(
            lambda o: tuple(a_sum[i].at[o, :, end] for end in ends),
            tuple(a_lastvia[i].at[:, end] for end in ends),
            tuple(tuple(a_last[i].at[d, :, end] for end in ends) for d in range(2)),
            y,
            y_peers,
        )
        step(a)
        step(b)
        for j in range(4):
            total = both[j, y, 16:32].astype(F32)
            for d in range(2):
                total = total + b_in[i][d, j].astype(F32)
            b_sum[i][j] = total.astype(BF16)
        b = ring_sum(
            lambda o: tuple(b_sum[i].at[o, :, end] for end in ends),
            tuple(b_lastvia[i].at[:, end] for end in ends),
            tuple(tuple(b_last[i].at[d, :, end] for end in ends) for d in range(2)),
            z,
            z_peers,
        )
        step(b)
        yield
        step(a, b)
        yield
        step(a, b)
        cols = slice(offset, offset + width)
        slab_out[0:16, cols] = (
            a_sum[i][y].astype(F32) + a_last[i][0].astype(F32) + a_last[i][1].astype(F32)
        )
        slab_out[16:32, cols] = (
            b_sum[i][z].astype(F32) + b_last[i][0].astype(F32) + b_last[i][1].astype(F32)
        )

    matrix_grad(wide2, gp16, 0)
    reduce_up = reduce(0)
    step(reduce_up, sum_g2)
    down_rows = partial_rows(act, DOWN, part_dn)
    down_rows(0)
    down_rows(1)
    matrix_grad(gwide, act, 1)
    reduce_down = reduce(1)
    step(reduce_down)

    def norm_back(total, unit, inv, gain):
        scaled = total * gain
        return inv * (scaled - row_mean(scaled) - unit * row_mean(scaled * unit))

    step(sum_g2)
    total = sum_rows(part_g2, in_g2)
    vsum[1:2] = jnp.sum(total * unit2[...], axis=0, keepdims=True)
    vsum[3:4] = jnp.sum(total, axis=0, keepdims=True)
    vsum[5:6] = jnp.sum(cot[...], axis=0, keepdims=True)
    grad_mid = cot[...] + norm_back(total, unit2[...], inv2[...], vec[1:2])
    g1[...] = grad_mid
    vsum[4:5] = jnp.sum(grad_mid, axis=0, keepdims=True)
    gawide[t] = grad_mid.astype(BF16)
    for n in range(4):
        cols = slice(n * 256, (n + 1) * 256)
        wcols = slice(2816 + n * 256, 2816 + (n + 1) * 256)
        out = dot(gawide[t], whole[:, :, :, :, wcols].reshape(1024, 256))
        gm_out[cols] = out.T.astype(BF16)
    gm_g = [
        make(
            gm_out.at[
                pl.ds(pl.multiple_of((around(t, dt) * 4 + around(k, dk)) * 64, 64), 64)
            ],
            gm_in.at[:, own_lanes(k, t)],
            member(dt, dk),
        )
        for dt, dk in group
    ]
    gm_in[:, own_lanes(k, t)] = gm_out[mine_rows]
    step(reduce_up, reduce_down)
    arrived(gm_g)
    gawide_x = ring_rows(gawide)
    step(reduce_up)
    gk_t[...] = jnp.zeros_like(gk_t)
    gv_t[...] = jnp.zeros_like(gv_t)

    def attend_back(first, begin, width):
        at = pl.ds(first, BLOCK)
        window = pl.ds(begin, width)
        p = jnp.exp(scores(first, begin, width) - lse[:, at])
        grad = gm_in[:, at]
        gv_t[:, window] += dot(grad, p.astype(BF16), NT)
        dp = dot(v_n[window], grad)
        centre = jnp.sum(p * dp, axis=0, keepdims=True)
        ds = (p * (dp - centre) * 0.125).astype(BF16)
        gq_t[:, at] = dot(k_t[:, window], ds).astype(BF16)
        gk_t[:, window] += dot(q_t[:, at], ds, NT)

    sum_dn = ring_sum_rows(part_dn, via_dn, in_dn)
    waiting = []

    def second():
        step(reduce_up, reduce_down)
        waiting.append(gawide_x())
        step(sum_dn)

    blocks(
        attend_back,
        second,
        lambda: step(reduce_up, reduce_down, sum_dn),
        lambda: step(reduce_up, reduce_down, sum_dn),
        lambda: None,
    )
    gawide_x = waiting[0]
    for j in range(4):
        span = slice(j * 512, (j + 1) * 512)
        gqkv_out[j, 0:64] = gq_t[:, span]
        gqkv_out[j, 64:128] = gk_t[:, span].astype(BF16)
        gqkv_out[j, 128:192] = gv_t[:, span].astype(BF16)
    back_c = [
        make(gqkv_out.at[around(k, d)], gqkv_in.at[k], ctx_peers[d - 1]) for d in STEPS
    ]
    gqkv_in[k] = gqkv_out[k]
    arrived(gawide_x)
    arrived(mixrows_c)
    gp16[:, 0:256] = mixrows_t[...].T
    matrix_grad(gawide, gp16.at[:, pl.ds(0, 256)], 2)
    reduce_out = reduce(2)
    step(reduce_out, reduce_up, reduce_down)
    r2_out[...] = r1[...] + sum_rows(part_dn, in_dn) + vec[5:6]
    arrived(back_c)
    gqkv[...] = gqkv_in[...].reshape(768, 512).T
    sum_g1 = ring_sum_rows(part_g1, via_g1, in_g1, partial_rows(gqkv, QKV, part_g1))
    step(sum_g1)
    step(reduce_out, reduce_down)
    sums = jnp.sum(gqkv[...].astype(F32), axis=0, keepdims=True)
    for i in range(6):
        tsum[i : i + 1] = sums[:, i * 128 : (i + 1) * 128]
    for i in range(8):
        tsum[6 + i : 7 + i] = bias_u[:, i * 128 : (i + 1) * 128]
    tsum[14:16] = jnp.zeros((2, 128), F32)
    matrix_grad(wide1, gqkv, 3)
    reduce_qkv = reduce(3)
    step(reduce_qkv, sum_g1, reduce_out)

    step(reduce_qkv)
    step(reduce_qkv)
    step(sum_g1)
    total = sum_rows(part_g1, in_g1)
    vsum[0:1] = jnp.sum(total * unit1[...], axis=0, keepdims=True)
    vsum[2:3] = jnp.sum(total, axis=0, keepdims=True)
    vsum[6:8] = jnp.zeros((2, 1024), F32)
    sum_z = [
        make(
            vsum.at[:, pl.ds(pl.multiple_of(around(z, d) * 256, 256), 256)],
            sz_vec.at[d - 1],
            z_peers[d - 1],
        )
        for d in STEPS
    ] + [make(tsum, sz_tp.at[d - 1], z_peers[d - 1]) for d in STEPS]
    step(reduce_qkv, reduce_out)
    g0_out[...] = g1[...] + norm_back(total, unit1[...], inv1[...], vec[0:1])
    arrived(sum_z)
    v1[...] = (
        vsum[:, pl.ds(pl.multiple_of(z * 256, 256), 256)] + sz_vec[0] + sz_vec[1] + sz_vec[2]
    )
    t1[...] = tsum[...] + sz_tp[0] + sz_tp[1] + sz_tp[2]
    s_y[0:8] = v1[:, pl.ds(pl.multiple_of((1 - yh) * 128, 128), 128)]
    s_y[8:24] = t1[...]
    sum_y = make(s_y, s_yin, opposite)
    step(reduce_qkv, reduce_out)
    sum_y.wait_recv()
    s_g[0:8] = v1[:, pl.ds(pl.multiple_of(yh * 128, 128), 128)] + s_yin[0:8]
    s_g[8:24] = t1[...] + s_yin[8:24]
    sum_c = [make(s_g, sg_c.at[d - 1], ctx_peers[d - 1]) for d in STEPS]
    sum_x = [
        make(s_g.at[pl.ds(0, 8)], sg_x.at[i], member(dt, dk)) for i, (dt, dk) in enumerate(far)
    ]
    step(reduce_qkv, reduce_out)
    step(reduce_qkv, reduce_out)
    step(reduce_up, reduce_down)
    arrived(sum_c)
    arrived(sum_x)
    total = s_g[...] + sg_c[0] + sg_c[1] + sg_c[2]
    norms = total[0:8]
    for i in range(12):
        norms = norms + sg_x[i]
    small_out[0:8] = norms
    small_out[8:24] = total[8:24]
    copies.finish()


COUNT = 336


def run_layer(*operands):
    vmem = pltpu.VMEM

    def per_chunk(*shape):
        return tuple(vmem((*shape, width), BF16) for _, width in CHUNKS)

    scratch = [
        vmem((4, 4, 2, 32, WIDE), BF16),
        vmem((24, 128), F32),
        vmem((1, 2048), F32),
        vmem((3, 24, 128), F32),
        vmem((12, 8, 128), F32),
        vmem((24, 128), F32),
        vmem((3, 24, 128), F32),
        vmem((6, 8, 128), F32),
        vmem((6, 8, 128), F32),
        vmem((8, 1024), F32),
        vmem((1, 768), F32),
        vmem((1, 1024), F32),
        vmem((4, 128, 1024), BF16),
        vmem((4, 128, 1024), BF16),
        vmem((4, 128, 1024), BF16),
        vmem((4, 128, 1024), BF16),
        vmem((128, 1024), F32),
        vmem((128, 1024), F32),
        vmem((128, 1), F32),
        vmem((128, 1), F32),
        vmem((128, 1024), F32),
        vmem((128, 1024), F32),
        vmem((768, 512), BF16),
        vmem((4, 192, 512), BF16),
        vmem((64, 2048), BF16),
        vmem((64, 2048), BF16),
        vmem((64, 2048), BF16),
        vmem((2048, 64), BF16),
        vmem((2048, 64), BF16),
        vmem((64, 2048), BF16),
        vmem((1, 2048), F32),
        vmem((1024, 128), BF16),
        vmem((256, 512), BF16),
        vmem((512, 1024), F32),
        vmem((512, 1024), BF16),
        vmem((512, 1024), BF16),
        vmem((4, 128, 1024), BF16),
        vmem((2, 128, 512), BF16),
        vmem((2, 128, 1024), BF16),
        vmem((4, 128, 1024), BF16),
        vmem((2, 128, 512), BF16),
        vmem((2, 128, 1024), BF16),
        vmem((4, 128, 1024), BF16),
        vmem((2, 128, 512), BF16),
        vmem((2, 128, 1024), BF16),
        vmem((1024, 128), BF16),
        vmem((64, 2048), BF16),
        vmem((64, 2048), BF16),
        vmem((64, 2048), F32),
        vmem((64, 2048), F32),
        vmem((4, 192, 512), BF16),
        vmem((4, 192, 512), BF16),
        vmem((512, 768), BF16),
        per_chunk(4, 4, 2, 32),
        per_chunk(4, 4, 32),
        per_chunk(4, 16),
        per_chunk(4, 16),
        per_chunk(2, 4, 16),
        per_chunk(2, 4, 16),
        per_chunk(4, 16),
        per_chunk(4, 16),
        per_chunk(16),
        per_chunk(16),
        per_chunk(2, 16),
        per_chunk(2, 16),
        vmem((8, 1024), F32),
        vmem((16, 128), F32),
        vmem((3, 8, 256), F32),
        vmem((3, 16, 128), F32),
        vmem((8, 256), F32),
        vmem((16, 128), F32),
        vmem((24, 128), F32),
        vmem((24, 128), F32),
        vmem((24, 128), F32),
        vmem((3, 24, 128), F32),
        vmem((12, 8, 128), F32),
        pltpu.SemaphoreType.DMA((COUNT,)),
        pltpu.SemaphoreType.DMA((COUNT,)),
    ]
    whole_vmem = pl.BlockSpec(memory_space=pltpu.VMEM)
    return pl.pallas_call(
        layer_kernel,
        out_shape=(
            jax.ShapeDtypeStruct((128, 1024), F32),
            jax.ShapeDtypeStruct((128, 1024), F32),
            jax.ShapeDtypeStruct((32, SLAB), F32),
            jax.ShapeDtypeStruct((24, 128), F32),
        ),
        in_specs=[whole_vmem] * len(operands),
        out_specs=(whole_vmem,) * 4,
        scratch_shapes=scratch,
        compiler_params=pltpu.CompilerParams(
            collective_id=0, has_side_effects=True, vmem_limit_bytes=60 << 20
        ),
        name="layer",
    )(*operands)


def on_device(
    hidden_in,
    segment_ids,
    norm_gain,
    norm_bias,
    w_qkv,
    qv_bias,
    w_out,
    out_bias,
    w_up,
    up_bias,
    w_down,
    cotangent,
):
    f, k, t = lax.axis_index("fsdp"), lax.axis_index("ctx"), lax.axis_index("tp")
    hidden_out, grad_input, out, sums = run_layer(
        w_up,
        w_down,
        w_qkv,
        w_out,
        norm_gain,
        norm_bias,
        out_bias,
        qv_bias,
        up_bias,
        hidden_in,
        cotangent,
        segment_ids,
    )

    norm_sums = lax.dynamic_slice_in_dim(sums[0:6], (k * 4 + t) * 8, 8, 1)
    qkv_sums = sums[8:14].reshape(4, 3, 64)
    qv_sums = lax.dynamic_slice_in_dim(
        jnp.stack([qkv_sums[:, 0], qkv_sums[:, 2]]), (f * 4 + k) * 2, 2, 2
    )
    up_sums = lax.dynamic_slice_in_dim(sums[14:22].reshape(4, 256), (f * 4 + k) * 8, 8, 1)
    return (
        hidden_out,
        grad_input,
        norm_sums[0:2].reshape(1, 2, 8),
        norm_sums[2:4].reshape(1, 2, 8),
        out[:, 2048:2816].reshape(32, 4, 3, 64).transpose(2, 0, 1, 3).reshape(1, 3, 32, 256),
        qv_sums.reshape(1, 2, 4, 2),
        out[:, 2816:3072].reshape(1, 32, 256),
        norm_sums[4:6].reshape(1, 2, 8),
        out[:, 0:1024].reshape(1, 32, 1024),
        up_sums.reshape(1, 4, 8),
        out[:, 1024:2048].reshape(1, 32, 1024),
    )


def solution(mesh):
    return jax.shard_map(
        on_device,
        mesh=mesh,
        in_specs=(
            P(("fsdp", "ctx", "tp"), None),
            P("fsdp", None),
            P(None, None, ("fsdp", "ctx", "tp")),
            P(None, None, ("fsdp", "ctx", "tp")),
            P(None, None, ("fsdp", "ctx"), "tp"),
            P(None, None, "tp", ("fsdp", "ctx")),
            P(None, ("fsdp", "ctx"), "tp"),
            P(None, None, ("fsdp", "ctx", "tp")),
            P(None, ("fsdp", "ctx"), "tp"),
            P(None, "tp", ("fsdp", "ctx")),
            P(None, ("fsdp", "ctx"), "tp"),
            P(("fsdp", "ctx", "tp"), None),
        ),
        out_specs=(
            P(("fsdp", "ctx", "tp"), None),
            P(("fsdp", "ctx", "tp"), None),
            P(None, None, ("fsdp", "ctx", "tp")),
            P(None, None, ("fsdp", "ctx", "tp")),
            P(None, None, ("fsdp", "ctx"), "tp"),
            P(None, None, "tp", ("fsdp", "ctx")),
            P(None, ("fsdp", "ctx"), "tp"),
            P(None, None, ("fsdp", "ctx", "tp")),
            P(None, ("fsdp", "ctx"), "tp"),
            P(None, "tp", ("fsdp", "ctx")),
            P(None, ("fsdp", "ctx"), "tp"),
        ),
        check_vma=False,
    )
```

```python
import jax
import jax.numpy as jnp
from jax import lax
from jax.experimental import pallas as pl
from jax.experimental.pallas import tpu as pltpu
from jax.sharding import PartitionSpec as P

H = 16
HD = 64
EPS = 1e-05
ROOT = 0.7978845608028654
CUBIC = 0.044715
NN = (((1,), (0,)), ((), ()))
NT = (((1,), (1,)), ((), ()))
TN = (((0,), (0,)), ((), ()))
MESH = pl.DeviceIdType.MESH
F32 = jnp.float32
BF16 = jnp.bfloat16
STEPS = (1, 2, 3)

QKV = slice(0, 768)
UP = slice(768, 1792)
DOWN = slice(1792, 2816)
OUT = slice(2816, 3840)
MLP = slice(768, 2816)
WIDE = 3840
SLAB = 3072
CHUNKS = ((0, 1024), (1024, 1024), (2816, 256), (2048, 768))
BLOCK = 256


def around(index, step):
    return lax.rem(index + step, 4)


def dot(a, b, dims=NN):
    return lax.dot_general(a, b, dims, preferred_element_type=F32)


class Copies:
    def __init__(self, send_sems, recv_sems):
        self.send_sems, self.recv_sems, self.used, self.all = send_sems, recv_sems, 0, []

    def make(self, src, dst, target):
        index = self.used
        self.used += 1
        assert index < COUNT
        copy = pltpu.make_async_remote_copy(
            src_ref=src,
            dst_ref=dst,
            send_sem=self.send_sems.at[index],
            recv_sem=self.recv_sems.at[index],
            device_id=target,
            device_id_type=MESH,
        )
        copy.start()
        self.all.append(copy)
        return copy

    def finish(self):
        for copy in self.all:
            copy.wait_send()


def step(*works):
    for work in works:
        next(work, None)


def arrived(copies):
    for copy in copies:
        copy.wait_recv()


def row_mean(x):
    return jnp.mean(x, axis=1, keepdims=True)


def layer_kernel(
    w_up,
    w_down,
    w_qkv_hbm,
    w_out,
    gain_in,
    shift_in,
    obias_in,
    qv_in,
    ub_in,
    hidden_hbm,
    cot_hbm,
    segments,
    r2_hbm,
    g0_hbm,
    qkv_hbm,
    out_hbm,
    up_hbm,
    down_hbm,
    gain_out,
    shift_out,
    obias_out,
    qv_out,
    ub_out,
    whole,
    w_qkv,
    hidden,
    cot,
    r2_out,
    g0_out,
    slab_out,
    slab_qkv,
    small,
    starts,
    near_c,
    near_x,
    tile_own,
    tile_z,
    pack_y,
    pack_yin,
    vec,
    bias_q,
    bias_u,
    wide1,
    gwide,
    wide2,
    gawide,
    unit1,
    unit2,
    inv1,
    inv2,
    r1,
    g1,
    qkv_out,
    qkv_in,
    q_t,
    k_t,
    v_t,
    k_n,
    v_n,
    out_t,
    lse,
    mix_t,
    mixrows_t,
    upre,
    act,
    gp16,
    part_g2,
    via_g2,
    in_g2,
    part_dn,
    via_dn,
    in_dn,
    part_g1,
    via_g1,
    in_g1,
    gm_out,
    gm_in,
    gq_t,
    gk_t,
    gv_t,
    gqkv_out,
    gqkv_in,
    gqkv,
    grads,
    core_in,
    a_via,
    b_via,
    a_in,
    b_in,
    a_sum,
    b_sum,
    a_lastvia,
    b_lastvia,
    a_last,
    b_last,
    vsum,
    tsum,
    sz_vec,
    sz_tp,
    v1,
    t1,
    s_y,
    s_yin,
    s_g,
    sg_c,
    sg_x,
    send_sems,
    recv_sems,
    local_sems,
):
    f, k, t = lax.axis_index("fsdp"), lax.axis_index("ctx"), lax.axis_index("tp")
    z, yh = f // 2, lax.rem(f, 2)
    yl, c = k // 2, lax.rem(k, 2)
    y = yh * 2 + yl
    head = t * 4 + k
    place = f * 4 + k
    slope = jnp.exp2(jnp.full((1, BLOCK), -8.0 / H, F32) * (head + 1).astype(F32))

    def at_zy(zz, yy, cc):
        return (zz * 2 + yy // 2, lax.rem(yy, 2) * 2 + cc, t)

    y_peers = [at_zy(z, around(y, d), c) for d in STEPS]
    z_peers = [at_zy(around(z, d), y, c) for d in STEPS]
    sibling = at_zy(z, y, 1 - c)
    opposite = at_zy(z, around(y, 2), c)
    ctx_peers = [(f, around(k, d), t) for d in STEPS]
    tp_peers = [(f, k, around(t, d)) for d in STEPS]
    group = [(dt, dk) for dt in range(4) for dk in range(4) if (dt, dk) != (0, 0)]

    def member(dt, dk):
        return (f, around(k, dk), around(t, dt))

    def move(index, src, dst):
        copy = pltpu.make_async_copy(src, dst, local_sems.at[index])
        copy.start()
        return copy

    own_out = pl.ds(pl.multiple_of(2816 + t * 256, 256), 256)
    qkv_load = move(0, w_qkv_hbm, w_qkv)
    out_load = move(1, w_out.at[0], whole.at[z, y, c, :, own_out])
    hidden_load = move(2, hidden_hbm, hidden)
    mlp_loads = [
        move(3, w_up.at[0], whole.at[z, y, c, :, 768:1792]),
        move(4, w_down.at[0], whole.at[z, y, c, :, 1792:2816]),
    ]
    cot_load = move(5, cot_hbm, cot)

    barrier = pltpu.get_barrier_semaphore()
    greeted = [member(dt, dk) for dt, dk in group] + y_peers + z_peers
    for partner in greeted:
        pl.semaphore_signal(barrier, inc=1, device_id=partner, device_id_type=MESH)
    pl.semaphore_wait(barrier, len(greeted))
    copies = Copies(send_sems, recv_sems)
    make = copies.make

    def lanes(count, period, index):
        row = lax.broadcasted_iota(jnp.int32, (count, 128), 0)
        lane = lax.broadcasted_iota(jnp.int32, (count, 128), 1)
        return ((lane % count == row) & ((lane % period) // count == index)).astype(F32)

    def scatter(values, hot):
        return lax.dot_general(
            values.astype(F32), hot, NN, precision=lax.Precision.HIGHEST, preferred_element_type=F32
        )

    small[...] = jnp.zeros_like(small)
    own = lanes(8, 128, k * 4 + t)
    small[0:2] = scatter(gain_in[0], own)
    small[2:4] = scatter(shift_in[0], own)
    small[4:6] = scatter(obias_in[0], own)
    pair = lanes(2, 64, place)
    left = lax.broadcasted_iota(jnp.int32, (4, 128), 1) < 64
    q_row, v_row = scatter(qv_in[0, 0], pair), scatter(qv_in[0, 1], pair)
    q_left, q_right = jnp.where(left, q_row, 0.0), jnp.where(left, 0.0, q_row)
    v_left, v_right = jnp.where(left, v_row, 0.0), jnp.where(left, 0.0, v_row)
    small[8:9] = q_left[0:1]
    small[9:10] = v_left[0:1] + q_right[1:2]
    small[10:11] = v_right[1:2]
    small[11:12] = q_left[2:3]
    small[12:13] = v_left[2:3] + q_right[3:4]
    small[13:14] = v_right[3:4]
    up_row = scatter(ub_in[0], lanes(8, 128, lax.rem(place, 16)))
    even = (place < 16).astype(F32)
    for i in range(4):
        small[14 + 2 * i : 15 + 2 * i] = up_row[i : i + 1] * even
        small[15 + 2 * i : 16 + 2 * i] = up_row[i : i + 1] * (1.0 - even)
    small_c = [make(small, near_c.at[d - 1], ctx_peers[d - 1]) for d in STEPS]
    far = [(dt, dk) for dt, dk in group if dt]
    small_x = [
        make(small.at[pl.ds(0, 8)], near_x.at[i], member(dt, dk)) for i, (dt, dk) in enumerate(far)
    ]

    upper, lower = pl.ds(0, 16), pl.ds(16, 16)
    low, high = pl.ds(0, 2), pl.ds(2, 2)

    def ring(part, me, peers):
        plus, minus = peers[0], peers[2]
        u, v = part(me)
        plus_u, minus_v = make(u, u, plus), make(v, v, minus)
        plus_v, minus_u = make(v, v, plus), make(u, u, minus)

        def forward():
            plus_u.wait_recv()
            u = part(around(me, 3))[0]
            next_u = make(u, u, plus)
            minus_v.wait_recv()
            v = part(around(me, 1))[1]
            return [plus_v, minus_u, next_u, make(v, v, minus)]

        return forward

    def ring_rows(buffer):
        return ring(
            lambda o: (buffer.at[o, :, pl.ds(0, 512)], buffer.at[o, :, pl.ds(512, 512)]),
            t,
            tp_peers,
        )

    def ring_sum(part, via, land, me, peers, filled=None):
        plus, minus = peers[0], peers[2]
        one, two, three = around(me, 1), around(me, 2), around(me, 3)
        if filled:
            filled(0)
        via_u = make(part(two)[0], via[0], plus)
        near_u = make(part(three)[0], land[1][0], minus)
        if filled:
            filled(1)
        via_v = make(part(two)[1], via[1], minus)
        near_v = make(part(one)[1], land[0][1], plus)
        yield
        via_u.wait_recv()
        via[0][...] = (via[0][...].astype(F32) + part(one)[0][...].astype(F32)).astype(BF16)
        next_u = make(via[0], land[0][0], plus)
        via_v.wait_recv()
        via[1][...] = (via[1][...].astype(F32) + part(three)[1][...].astype(F32)).astype(BF16)
        next_v = make(via[1], land[1][1], minus)
        yield
        arrived([near_u, near_v, next_u, next_v])

    def ring_sum_rows(part, via, land, filled=None):
        ends = pl.ds(0, 512), pl.ds(512, 512)
        return ring_sum(
            lambda o: tuple(part.at[o, :, end] for end in ends),
            (via.at[0], via.at[1]),
            tuple(tuple(land.at[i, :, end] for end in ends) for i in range(2)),
            t,
            tp_peers,
            filled,
        )

    def gather(cols):
        middle = (cols.start + cols.stop) // 2
        ends = slice(cols.start, middle), slice(middle, cols.stop)
        a = ring(lambda o: tuple(whole.at[z, o, c, upper, end] for end in ends), y, y_peers)
        b = ring(lambda o: tuple(whole.at[o, y, c, lower, end] for end in ends), z, z_peers)
        yield
        a, b = a(), b()
        yield
        arrived(a)
        a = ring(lambda o: tuple(whole.at[o, yy, c, upper, cols] for yy in (low, high)), z, z_peers)
        arrived(b)
        b = ring(lambda o: tuple(whole.at[zz, o, c, lower, cols] for zz in (low, high)), y, y_peers)

        def both(d):
            for block in (
                whole.at[around(z, d), :, c, upper, cols],
                whole.at[:, around(y, d), c, lower, cols],
            ):
                core.append(make(block, block, sibling))

        core = []
        both(0)
        yield
        a, b = a(), b()
        yield
        arrived(a + b)
        for d in STEPS:
            both(d)
        yield
        arrived(core)

    qkv_load.wait()
    for j in range(4):
        for i in range(3):
            col = j * 192 + i * 64
            whole[z, y, c, :, col : col + 64] = w_qkv[0, i, :, j * 64 : j * 64 + 64]
    gather_qkv = gather(QKV)
    step(gather_qkv)
    out_load.wait()
    out_cols = whole.at[z, y, c, :, own_out]
    out_x = [make(out_cols, out_cols, peer) for peer in tp_peers]
    hidden_load.wait()

    r = hidden[...].astype(F32)
    centered = r - row_mean(r)
    rstd = lax.rsqrt(row_mean(centered * centered) + EPS)
    unit1[...] = centered * rstd
    inv1[...] = rstd

    arrived(small_c)
    arrived(small_x)
    total = small[...] + near_c[0] + near_c[1] + near_c[2]
    norms = total[0:8]
    for i in range(12):
        norms = norms + near_x[i]
    tile_own[0:8] = norms
    tile_own[8:24] = total[8:24]
    small_z = [make(tile_own, tile_z.at[d - 1], z_peers[d - 1]) for d in STEPS]
    step(gather_qkv)
    arrived(small_z)
    pack_y[0] = tile_own[0:8]
    columns = tile_own[8:24]
    for d in STEPS:
        pack_y[d] = tile_z[d - 1, 0:8]
        columns = columns + tile_z[d - 1, 8:24]
    pack_y[4] = columns[0:8]
    pack_y[5] = columns[8:16]
    small_y = make(pack_y, pack_yin, opposite)
    step(gather_qkv)
    small_y.wait_recv()
    for d in range(4):
        origin = around(z, 4 - d) * 2
        vec[:, pl.ds(pl.multiple_of((origin + yh) * 128, 128), 128)] = pack_y[d]
        vec[:, pl.ds(pl.multiple_of((origin + 1 - yh) * 128, 128), 128)] = pack_yin[d]
    first_rows = pack_y[4] + pack_yin[4]
    later_rows = pack_y[5] + pack_yin[5]
    rows = [first_rows[i : i + 1] for i in range(8)] + [later_rows[i : i + 1] for i in range(6)]
    for i in range(6):
        bias_q[:, i * 128 : (i + 1) * 128] = rows[i]
    for i in range(8):
        bias_u[:, i * 128 : (i + 1) * 128] = rows[6 + i]

    wide1[t] = (unit1[...] * vec[0:1] + vec[2:3]).astype(BF16)
    wide1_x = ring_rows(wide1)
    step(gather_qkv)
    arrived(out_x)
    gather_out = gather(OUT)
    step(gather_out)
    wide1_x = wide1_x()
    cot_load.wait()
    gwide[t] = cot[...].astype(BF16)
    ids = segments[...]
    first = jnp.zeros((1, 2048), F32)
    for value in range(1, 4):
        count = jnp.sum((ids < value).astype(F32), axis=1, keepdims=True)
        first = jnp.where(ids >= value, count, first)
    starts[...] = first
    step(gather_qkv)
    step(gather_out)
    step(gather_qkv)
    arrived(wide1_x)
    gwide_x = ring_rows(gwide)

    def project(n, carry):
        cols = pl.ds(pl.multiple_of(n * 256, 256), 256)
        out = dot(wide1[...].reshape(512, 1024), whole[:, :, :, :, cols].reshape(1024, 256))
        qkv_out[cols] = (out + bias_q[:, cols]).T.astype(BF16)
        return carry

    lax.fori_loop(0, 3, project, 0)

    def head_rows(j):
        return pl.ds(pl.multiple_of(j * 192, 64), 192)

    heads_c = [
        make(qkv_out.at[head_rows(around(k, d))], qkv_in.at[k], ctx_peers[d - 1]) for d in STEPS
    ]
    qkv_in[k] = qkv_out[head_rows(k)]
    step(gather_out)
    gwide_x = gwide_x()
    step(gather_out)
    arrived(heads_c)
    for copy in mlp_loads:
        copy.wait()
    gather_mlp = gather(MLP)
    step(gather_mlp)
    for i in range(4):
        span = slice(i * 512, (i + 1) * 512)
        q_t[:, span] = qkv_in[i, 0:64]
        keys = qkv_in[i, 64:128]
        values = qkv_in[i, 128:192]
        k_t[:, span] = keys
        v_t[:, span] = values
        k_n[span] = keys.T
        v_n[span] = values.T

    def scores(first, begin, width):
        at = pl.ds(first, BLOCK)
        s = dot(k_n[pl.ds(begin, width)], q_t[:, at])
        key = begin + lax.broadcasted_iota(jnp.int32, (width, BLOCK), 0)
        query = first + lax.broadcasted_iota(jnp.int32, (width, BLOCK), 1)
        s = s * 0.125 + slope * (key - first).astype(F32)
        return jnp.where((key <= query) & (key.astype(F32) >= starts[:, at]), s, -jnp.inf)

    def attend(first, begin, width):
        at = pl.ds(first, BLOCK)
        s = scores(first, begin, width)
        highest = jnp.max(s, axis=0, keepdims=True)
        e = jnp.exp(s - highest)
        totals = jnp.sum(e, axis=0, keepdims=True)
        probs = (e * (1.0 / totals)).astype(BF16)
        out_t[:, at] = dot(v_t[:, pl.ds(begin, width)], probs).astype(BF16)
        lse[:, at] = highest + jnp.log(totals)

    def blocks(body, *between):
        def later(b, carry):
            begin = pl.multiple_of(b * BLOCK, BLOCK)
            body(pl.multiple_of(begin + 1024, BLOCK), begin, 1024 + BLOCK)
            return carry

        for b in range(4):
            body(b * BLOCK, 0, (b + 1) * BLOCK)
            if b == 1:
                between[0]()
        between[1]()
        lax.fori_loop(0, 2, later, 0)
        between[2]()
        lax.fori_loop(2, 4, later, 0)
        between[3]()

    blocks(
        attend,
        lambda: step(gather_out, gather_mlp),
        lambda: step(gather_mlp),
        lambda: step(gather_mlp),
        lambda: None,
    )

    def own_lanes(kk, tt):
        return pl.ds(pl.multiple_of(kk * 512 + tt * 128, 128), 128)

    mine_rows = pl.ds(pl.multiple_of(head * 64, 64), 64)
    mix_g = [
        make(out_t.at[:, own_lanes(around(k, dk), around(t, dt))], mix_t.at[mine_rows], member(dt, dk))
        for dt, dk in group
    ]
    mix_t[mine_rows] = out_t[:, own_lanes(k, t)]
    step(gather_out, gather_mlp)
    arrived(mix_g)
    local_rows = pl.ds(pl.multiple_of(k * 64, 64), 64)
    mixrows_c = [
        make(
            out_t.at[:, pl.ds(pl.multiple_of(around(k, d) * 512, 512), 512)],
            mixrows_t.at[local_rows],
            ctx_peers[d - 1],
        )
        for d in STEPS
    ]
    mixrows_t[local_rows] = out_t[:, pl.ds(pl.multiple_of(k * 512, 512), 512)]

    for n in range(4):
        cols = slice(n * 256, (n + 1) * 256)
        out = dot(whole[n, :, :, :, OUT].reshape(256, 1024), mix_t[...])
        r1[:, cols] = hidden[:, cols].astype(F32) + out.T + vec[4:5, cols]
    r = r1[...]
    centered = r - row_mean(r)
    rstd = lax.rsqrt(row_mean(centered * centered) + EPS)
    unit2[...] = centered * rstd
    inv2[...] = rstd
    wide2[t] = (unit2[...] * vec[1:2] + vec[3:4]).astype(BF16)
    wide2_x = ring_rows(wide2)
    step(gather_mlp)
    arrived(gwide_x)

    def pull(n, carry):
        cols = pl.ds(pl.multiple_of(n * 256, 256), 256)
        wcols = pl.ds(pl.multiple_of(1792 + n * 256, 256), 256)
        upre[:, cols] = dot(
            gwide[...].reshape(512, 1024), whole[:, :, :, :, wcols].reshape(1024, 256)
        )
        return carry

    lax.fori_loop(0, 2, pull, 0)
    wide2_x = wide2_x()
    lax.fori_loop(2, 4, pull, 0)
    arrived(wide2_x)

    def feed(n, carry):
        cols = pl.ds(pl.multiple_of(n * 256, 256), 256)
        wcols = pl.ds(pl.multiple_of(768 + n * 256, 256), 256)
        pre = (
            dot(wide2[...].reshape(512, 1024), whole[:, :, :, :, wcols].reshape(1024, 256))
            + bias_u[:, cols]
        )
        curve = jnp.tanh(ROOT * (pre + CUBIC * pre * pre * pre))
        act[:, cols] = (0.5 * pre * (1.0 + curve)).astype(BF16)
        slant = 0.5 * (1.0 + curve) + 0.5 * pre * (1.0 - curve * curve) * ROOT * (
            1.0 + 3.0 * CUBIC * pre * pre
        )
        gpre = upre[:, cols] * slant
        gp16[:, cols] = gpre.astype(BF16)
        bias_u[:, cols] = jnp.sum(gpre, axis=0, keepdims=True)
        return carry

    lax.fori_loop(0, 4, feed, 0)

    def partial_rows(source, cols, part):
        def one(n, carry):
            width = cols.stop - cols.start
            out = dot(source[...], whole[n, :, :, :, cols].reshape(256, width), NT)
            part[:, :, pl.ds(pl.multiple_of(n * 256, 256), 256)] = out.astype(BF16).reshape(
                4, 128, 256
            )
            return carry

        return lambda half: lax.fori_loop(2 * half, 2 * half + 2, one, 0)

    def sum_rows(part, landing):
        return part[t].astype(F32) + landing[0].astype(F32) + landing[1].astype(F32)

    sum_g2 = ring_sum_rows(part_g2, via_g2, in_g2, partial_rows(gp16, UP, part_g2))
    step(sum_g2)

    def matrix_grad(left, right, chunk):
        width = CHUNKS[chunk][1]

        def one(m, carry):
            rows = left[:, :, pl.ds(pl.multiple_of(m * 256, 256), 256)].reshape(512, 256)
            out = dot(rows, right[...], TN)
            grads[chunk][m] = out.astype(BF16).reshape(4, 2, 32, width)
            return carry

        lax.fori_loop(0, 4, one, 0)

    def reduce(i):
        offset, width = CHUNKS[i]
        both = core_in[i]
        core = make(grads[i].at[:, :, 1 - c], both, sibling)
        yield
        core.wait_recv()

        def add(j, carry):
            zz, yy = j // 4, lax.rem(j, 4)
            total = grads[i][zz, yy, c].astype(F32) + both[zz, yy].astype(F32)
            both[zz, yy] = total.astype(BF16)
            return carry

        lax.fori_loop(0, 16, add, 0)
        yield
        a = ring_sum(
            lambda o: (both.at[o, low, upper], both.at[o, high, upper]),
            (a_via[i].at[low], a_via[i].at[high]),
            tuple((a_in[i].at[d, low], a_in[i].at[d, high]) for d in range(2)),
            z,
            z_peers,
        )
        b = ring_sum(
            lambda o: (both.at[low, o, lower], both.at[high, o, lower]),
            (b_via[i].at[low], b_via[i].at[high]),
            tuple((b_in[i].at[d, low], b_in[i].at[d, high]) for d in range(2)),
            y,
            y_peers,
        )
        step(a, b)
        yield
        step(a, b)
        yield
        step(a)
        for j in range(4):
            total = both[z, j, 0:16].astype(F32)
            for d in range(2):
                total = total + a_in[i][d, j].astype(F32)
            a_sum[i][j] = total.astype(BF16)
        ends = pl.ds(0, width // 2), pl.ds(width // 2, width // 2)
        a = ring_sum(
            lambda o: tuple(a_sum[i].at[o, :, end] for end in ends),
            tuple(a_lastvia[i].at[:, end] for end in ends),
            tuple(tuple(a_last[i].at[d, :, end] for end in ends) for d in range(2)),
            y,
            y_peers,
        )
        step(a)
        step(b)
        for j in range(4):
            total = both[j, y, 16:32].astype(F32)
            for d in range(2):
                total = total + b_in[i][d, j].astype(F32)
            b_sum[i][j] = total.astype(BF16)
        b = ring_sum(
            lambda o: tuple(b_sum[i].at[o, :, end] for end in ends),
            tuple(b_lastvia[i].at[:, end] for end in ends),
            tuple(tuple(b_last[i].at[d, :, end] for end in ends) for d in range(2)),
            z,
            z_peers,
        )
        step(b)
        yield
        step(a, b)
        yield
        step(a, b)
        cols = slice(offset, offset + width)
        slab_out[0:16, cols] = (
            a_sum[i][y].astype(F32) + a_last[i][0].astype(F32) + a_last[i][1].astype(F32)
        )
        slab_out[16:32, cols] = (
            b_sum[i][z].astype(F32) + b_last[i][0].astype(F32) + b_last[i][1].astype(F32)
        )

    matrix_grad(wide2, gp16, 0)
    reduce_up = reduce(0)
    step(reduce_up, sum_g2)
    down_rows = partial_rows(act, DOWN, part_dn)
    down_rows(0)
    down_rows(1)
    matrix_grad(gwide, act, 1)
    reduce_down = reduce(1)
    step(reduce_down)

    def norm_back(total, unit, inv, gain):
        scaled = total * gain
        return inv * (scaled - row_mean(scaled) - unit * row_mean(scaled * unit))

    step(sum_g2)
    total = sum_rows(part_g2, in_g2)
    vsum[1:2] = jnp.sum(total * unit2[...], axis=0, keepdims=True)
    vsum[3:4] = jnp.sum(total, axis=0, keepdims=True)
    vsum[5:6] = jnp.sum(cot[...], axis=0, keepdims=True)
    grad_mid = cot[...] + norm_back(total, unit2[...], inv2[...], vec[1:2])
    g1[...] = grad_mid
    vsum[4:5] = jnp.sum(grad_mid, axis=0, keepdims=True)
    gawide[t] = grad_mid.astype(BF16)
    for n in range(4):
        cols = slice(n * 256, (n + 1) * 256)
        wcols = slice(2816 + n * 256, 2816 + (n + 1) * 256)
        out = dot(gawide[t], whole[:, :, :, :, wcols].reshape(1024, 256))
        gm_out[cols] = out.T.astype(BF16)
    gm_g = [
        make(
            gm_out.at[
                pl.ds(pl.multiple_of((around(t, dt) * 4 + around(k, dk)) * 64, 64), 64)
            ],
            gm_in.at[:, own_lanes(k, t)],
            member(dt, dk),
        )
        for dt, dk in group
    ]
    gm_in[:, own_lanes(k, t)] = gm_out[mine_rows]
    step(reduce_up, reduce_down)
    arrived(gm_g)
    gawide_x = ring_rows(gawide)
    step(reduce_up)
    gk_t[...] = jnp.zeros_like(gk_t)
    gv_t[...] = jnp.zeros_like(gv_t)

    def attend_back(first, begin, width):
        at = pl.ds(first, BLOCK)
        window = pl.ds(begin, width)
        p = jnp.exp(scores(first, begin, width) - lse[:, at])
        grad = gm_in[:, at]
        gv_t[:, window] += dot(grad, p.astype(BF16), NT)
        dp = dot(v_n[window], grad)
        centre = jnp.sum(p * dp, axis=0, keepdims=True)
        ds = (p * (dp - centre) * 0.125).astype(BF16)
        gq_t[:, at] = dot(k_t[:, window], ds).astype(BF16)
        gk_t[:, window] += dot(q_t[:, at], ds, NT)

    sum_dn = ring_sum_rows(part_dn, via_dn, in_dn)
    waiting = []

    def second():
        step(reduce_up, reduce_down)
        waiting.append(gawide_x())
        step(sum_dn)

    blocks(
        attend_back,
        second,
        lambda: step(reduce_up, reduce_down, sum_dn),
        lambda: step(reduce_up, reduce_down, sum_dn),
        lambda: None,
    )
    gawide_x = waiting[0]
    for j in range(4):
        span = slice(j * 512, (j + 1) * 512)
        gqkv_out[j, 0:64] = gq_t[:, span]
        gqkv_out[j, 64:128] = gk_t[:, span].astype(BF16)
        gqkv_out[j, 128:192] = gv_t[:, span].astype(BF16)
    back_c = [
        make(gqkv_out.at[around(k, d)], gqkv_in.at[k], ctx_peers[d - 1]) for d in STEPS
    ]
    gqkv_in[k] = gqkv_out[k]
    arrived(gawide_x)
    arrived(mixrows_c)
    gp16[:, 0:256] = mixrows_t[...].T
    matrix_grad(gawide, gp16.at[:, pl.ds(0, 256)], 2)
    reduce_out = reduce(2)
    step(reduce_out, reduce_up, reduce_down)
    r2_out[...] = r1[...] + sum_rows(part_dn, in_dn) + vec[5:6]
    stores = [move(6, r2_out, r2_hbm)]
    arrived(back_c)
    gqkv[...] = gqkv_in[...].reshape(768, 512).T
    sum_g1 = ring_sum_rows(part_g1, via_g1, in_g1, partial_rows(gqkv, QKV, part_g1))
    step(sum_g1)
    step(reduce_out, reduce_down)
    sums = jnp.sum(gqkv[...].astype(F32), axis=0, keepdims=True)
    for i in range(6):
        tsum[i : i + 1] = sums[:, i * 128 : (i + 1) * 128]
    for i in range(8):
        tsum[6 + i : 7 + i] = bias_u[:, i * 128 : (i + 1) * 128]
    tsum[14:16] = jnp.zeros((2, 128), F32)
    matrix_grad(wide1, gqkv, 3)
    reduce_qkv = reduce(3)
    step(reduce_qkv, sum_g1, reduce_out)

    step(reduce_qkv)
    step(reduce_qkv)
    step(sum_g1)
    total = sum_rows(part_g1, in_g1)
    vsum[0:1] = jnp.sum(total * unit1[...], axis=0, keepdims=True)
    vsum[2:3] = jnp.sum(total, axis=0, keepdims=True)
    vsum[6:8] = jnp.zeros((2, 1024), F32)
    sum_z = [
        make(
            vsum.at[:, pl.ds(pl.multiple_of(around(z, d) * 256, 256), 256)],
            sz_vec.at[d - 1],
            z_peers[d - 1],
        )
        for d in STEPS
    ] + [make(tsum, sz_tp.at[d - 1], z_peers[d - 1]) for d in STEPS]
    step(reduce_qkv, reduce_out)
    g0_out[...] = g1[...] + norm_back(total, unit1[...], inv1[...], vec[0:1])
    stores.append(move(7, g0_out, g0_hbm))
    arrived(sum_z)
    v1[...] = (
        vsum[:, pl.ds(pl.multiple_of(z * 256, 256), 256)] + sz_vec[0] + sz_vec[1] + sz_vec[2]
    )
    t1[...] = tsum[...] + sz_tp[0] + sz_tp[1] + sz_tp[2]
    s_y[0:8] = v1[:, pl.ds(pl.multiple_of((1 - yh) * 128, 128), 128)]
    s_y[8:24] = t1[...]
    sum_y = make(s_y, s_yin, opposite)
    step(reduce_qkv, reduce_out)
    sum_y.wait_recv()
    s_g[0:8] = v1[:, pl.ds(pl.multiple_of(yh * 128, 128), 128)] + s_yin[0:8]
    s_g[8:24] = t1[...] + s_yin[8:24]
    sum_c = [make(s_g, sg_c.at[d - 1], ctx_peers[d - 1]) for d in STEPS]
    sum_x = [
        make(s_g.at[pl.ds(0, 8)], sg_x.at[i], member(dt, dk)) for i, (dt, dk) in enumerate(far)
    ]
    step(reduce_qkv, reduce_out)
    step(reduce_qkv, reduce_out)
    step(reduce_up, reduce_down)
    for j in range(4):
        for i in range(3):
            col = 2048 + j * 192 + i * 64
            slab_qkv[0, i, :, j * 64 : j * 64 + 64] = slab_out[:, col : col + 64]
    stores += [
        move(8, slab_qkv, qkv_hbm),
        move(9, slab_out.at[:, 2816:3072], out_hbm.at[0]),
        move(10, slab_out.at[:, 0:1024], up_hbm.at[0]),
        move(11, slab_out.at[:, 1024:2048], down_hbm.at[0]),
    ]
    arrived(sum_c)
    arrived(sum_x)
    total = s_g[...] + sg_c[0] + sg_c[1] + sg_c[2]
    norms = total[0:8]
    for i in range(12):
        norms = norms + sg_x[i]
    def pick(values, hot):
        return lax.dot_general(
            values, hot, NT, precision=lax.Precision.HIGHEST, preferred_element_type=F32
        )

    mine = pick(norms, own)
    gain_out[0] = mine[0:2]
    shift_out[0] = mine[2:4]
    obias_out[0] = mine[4:6]
    left = lax.broadcasted_iota(jnp.int32, (2, 128), 1) < 64
    from_left = pick(total[8:24], jnp.where(left, pair, 0.0))
    from_right = pick(total[8:24], jnp.where(left, 0.0, pair))
    qv_out[0, 0, 0:1] = from_left[0:1]
    qv_out[0, 0, 1:2] = from_right[1:2]
    qv_out[0, 0, 2:3] = from_left[3:4]
    qv_out[0, 0, 3:4] = from_right[4:5]
    qv_out[0, 1, 0:1] = from_left[1:2]
    qv_out[0, 1, 1:2] = from_right[2:3]
    qv_out[0, 1, 2:3] = from_left[4:5]
    qv_out[0, 1, 3:4] = from_right[5:6]
    ups = pick(total[8:24], lanes(8, 128, lax.rem(place, 16)))
    for i in range(4):
        ub_out[0, i : i + 1] = (
            ups[6 + 2 * i : 7 + 2 * i] * even + ups[7 + 2 * i : 8 + 2 * i] * (1.0 - even)
        )
    for copy in stores:
        copy.wait()
    copies.finish()


def place_kernel(*refs):
    count = (len(refs) - 1) // 2
    sems = refs[-1]
    copies = []
    for i, (src, dst) in enumerate(zip(refs[:count], refs[count : 2 * count])):
        if i < 6:
            copy = pltpu.make_async_copy(src, dst, sems.at[i])
            copy.start()
            copies.append(copy)
        else:
            dst[...] = src[...]
    for copy in copies:
        copy.wait()


OUTPUTS = (
    (128, 1024),
    (128, 1024),
    (1, 3, 32, 256),
    (1, 32, 256),
    (1, 32, 1024),
    (1, 32, 1024),
    (1, 2, 8),
    (1, 2, 8),
    (1, 2, 8),
    (1, 2, 4, 2),
    (1, 4, 8),
)
COUNT = 336


def run_layer(*operands):
    vmem = pltpu.VMEM

    def per_chunk(*shape):
        return tuple(vmem((*shape, width), BF16) for _, width in CHUNKS)

    scratch = [
        vmem((4, 4, 2, 32, WIDE), BF16),
        vmem((1, 3, 32, 256), BF16),
        vmem((128, 1024), BF16),
        vmem((128, 1024), F32),
        vmem((128, 1024), F32),
        vmem((128, 1024), F32),
        vmem((32, SLAB), F32),
        vmem((1, 3, 32, 256), F32),
        vmem((24, 128), F32),
        vmem((1, 2048), F32),
        vmem((3, 24, 128), F32),
        vmem((12, 8, 128), F32),
        vmem((24, 128), F32),
        vmem((3, 24, 128), F32),
        vmem((6, 8, 128), F32),
        vmem((6, 8, 128), F32),
        vmem((8, 1024), F32),
        vmem((1, 768), F32),
        vmem((1, 1024), F32),
        vmem((4, 128, 1024), BF16),
        vmem((4, 128, 1024), BF16),
        vmem((4, 128, 1024), BF16),
        vmem((4, 128, 1024), BF16),
        vmem((128, 1024), F32),
        vmem((128, 1024), F32),
        vmem((128, 1), F32),
        vmem((128, 1), F32),
        vmem((128, 1024), F32),
        vmem((128, 1024), F32),
        vmem((768, 512), BF16),
        vmem((4, 192, 512), BF16),
        vmem((64, 2048), BF16),
        vmem((64, 2048), BF16),
        vmem((64, 2048), BF16),
        vmem((2048, 64), BF16),
        vmem((2048, 64), BF16),
        vmem((64, 2048), BF16),
        vmem((1, 2048), F32),
        vmem((1024, 128), BF16),
        vmem((256, 512), BF16),
        vmem((512, 1024), F32),
        vmem((512, 1024), BF16),
        vmem((512, 1024), BF16),
        vmem((4, 128, 1024), BF16),
        vmem((2, 128, 512), BF16),
        vmem((2, 128, 1024), BF16),
        vmem((4, 128, 1024), BF16),
        vmem((2, 128, 512), BF16),
        vmem((2, 128, 1024), BF16),
        vmem((4, 128, 1024), BF16),
        vmem((2, 128, 512), BF16),
        vmem((2, 128, 1024), BF16),
        vmem((1024, 128), BF16),
        vmem((64, 2048), BF16),
        vmem((64, 2048), BF16),
        vmem((64, 2048), F32),
        vmem((64, 2048), F32),
        vmem((4, 192, 512), BF16),
        vmem((4, 192, 512), BF16),
        vmem((512, 768), BF16),
        per_chunk(4, 4, 2, 32),
        per_chunk(4, 4, 32),
        per_chunk(4, 16),
        per_chunk(4, 16),
        per_chunk(2, 4, 16),
        per_chunk(2, 4, 16),
        per_chunk(4, 16),
        per_chunk(4, 16),
        per_chunk(16),
        per_chunk(16),
        per_chunk(2, 16),
        per_chunk(2, 16),
        vmem((8, 1024), F32),
        vmem((16, 128), F32),
        vmem((3, 8, 256), F32),
        vmem((3, 16, 128), F32),
        vmem((8, 256), F32),
        vmem((16, 128), F32),
        vmem((24, 128), F32),
        vmem((24, 128), F32),
        vmem((24, 128), F32),
        vmem((3, 24, 128), F32),
        vmem((12, 8, 128), F32),
        pltpu.SemaphoreType.DMA((COUNT,)),
        pltpu.SemaphoreType.DMA((COUNT,)),
        pltpu.SemaphoreType.DMA((12,)),
    ]
    in_vmem, in_place = pl.BlockSpec(memory_space=pltpu.VMEM), pl.BlockSpec(memory_space=pl.ANY)
    shapes = tuple(jax.ShapeDtypeStruct(shape, F32) for shape in OUTPUTS)
    places = (in_place,) * 6 + (in_vmem,) * 5
    results = pl.pallas_call(
        layer_kernel,
        out_shape=shapes,
        in_specs=[in_place] * 4 + [in_vmem] * 5 + [in_place] * 2 + [in_vmem],
        out_specs=places,
        scratch_shapes=scratch,
        compiler_params=pltpu.CompilerParams(
            collective_id=0, has_side_effects=True, vmem_limit_bytes=60 << 20
        ),
        name="layer",
    )(*operands)
    return pl.pallas_call(
        place_kernel,
        out_shape=shapes,
        in_specs=list(places),
        out_specs=places,
        scratch_shapes=[pltpu.SemaphoreType.DMA((6,))],
        name="place",
    )(*results)


def on_device(
    hidden_in,
    segment_ids,
    norm_gain,
    norm_bias,
    w_qkv,
    qv_bias,
    w_out,
    out_bias,
    w_up,
    up_bias,
    w_down,
    cotangent,
):
    hidden_out, grad_input, qkv, out, up, down, gain, shift, obias, qv, ub = run_layer(
        w_up,
        w_down,
        w_qkv,
        w_out,
        norm_gain,
        norm_bias,
        out_bias,
        qv_bias,
        up_bias,
        hidden_in,
        cotangent,
        segment_ids,
    )
    return hidden_out, grad_input, gain, shift, qkv, qv, out, obias, up, ub, down


def solution(mesh):
    return jax.shard_map(
        on_device,
        mesh=mesh,
        in_specs=(
            P(("fsdp", "ctx", "tp"), None),
            P("fsdp", None),
            P(None, None, ("fsdp", "ctx", "tp")),
            P(None, None, ("fsdp", "ctx", "tp")),
            P(None, None, ("fsdp", "ctx"), "tp"),
            P(None, None, "tp", ("fsdp", "ctx")),
            P(None, ("fsdp", "ctx"), "tp"),
            P(None, None, ("fsdp", "ctx", "tp")),
            P(None, ("fsdp", "ctx"), "tp"),
            P(None, "tp", ("fsdp", "ctx")),
            P(None, ("fsdp", "ctx"), "tp"),
            P(("fsdp", "ctx", "tp"), None),
        ),
        out_specs=(
            P(("fsdp", "ctx", "tp"), None),
            P(("fsdp", "ctx", "tp"), None),
            P(None, None, ("fsdp", "ctx", "tp")),
            P(None, None, ("fsdp", "ctx", "tp")),
            P(None, None, ("fsdp", "ctx"), "tp"),
            P(None, None, "tp", ("fsdp", "ctx")),
            P(None, ("fsdp", "ctx"), "tp"),
            P(None, None, ("fsdp", "ctx", "tp")),
            P(None, ("fsdp", "ctx"), "tp"),
            P(None, "tp", ("fsdp", "ctx")),
            P(None, ("fsdp", "ctx"), "tp"),
        ),
        check_vma=False,
    )
```

```python
import jax
import jax.numpy as jnp
from jax import lax
from jax.experimental import pallas as pl
from jax.experimental.pallas import tpu as pltpu
from jax.sharding import PartitionSpec as P

H = 16
HD = 64
EPS = 1e-05
ROOT = 0.7978845608028654
CUBIC = 0.044715
NN = (((1,), (0,)), ((), ()))
NT = (((1,), (1,)), ((), ()))
TN = (((0,), (0,)), ((), ()))
MESH = pl.DeviceIdType.MESH
F32 = jnp.float32
BF16 = jnp.bfloat16
STEPS = (1, 2, 3)

QKV = slice(0, 768)
UP = slice(768, 1792)
DOWN = slice(1792, 2816)
OUT = slice(2816, 3840)
MLP = slice(768, 2816)
WIDE = 3840
SLAB = 3072
CHUNKS = ((0, 1024), (1024, 1024), (2816, 256), (2048, 768))
BLOCK = 256


def around(index, step):
    return lax.rem(index + step, 4)


def dot(a, b, dims=NN):
    return lax.dot_general(a, b, dims, preferred_element_type=F32)


class Copies:
    def __init__(self, send_sems, recv_sems):
        self.send_sems, self.recv_sems, self.used, self.all = send_sems, recv_sems, 0, []

    def make(self, src, dst, target):
        index = self.used
        self.used += 1
        assert index < COUNT
        copy = pltpu.make_async_remote_copy(
            src_ref=src,
            dst_ref=dst,
            send_sem=self.send_sems.at[index],
            recv_sem=self.recv_sems.at[index],
            device_id=target,
            device_id_type=MESH,
        )
        copy.start()
        self.all.append(copy)
        return copy

    def finish(self):
        for copy in self.all:
            copy.wait_send()


def step(*works):
    for work in works:
        next(work, None)


def arrived(copies):
    for copy in copies:
        copy.wait_recv()


def row_mean(x):
    return jnp.mean(x, axis=1, keepdims=True)


def layer_kernel(
    w_up,
    w_down,
    w_qkv_hbm,
    w_out,
    gain_in,
    shift_in,
    obias_in,
    qv_in,
    ub_in,
    hidden_hbm,
    cot_hbm,
    segments,
    r2_hbm,
    g0_hbm,
    qkv_hbm,
    out_hbm,
    up_hbm,
    down_hbm,
    gain_out,
    shift_out,
    obias_out,
    qv_out,
    ub_out,
    whole,
    w_qkv,
    hidden,
    cot,
    r2_out,
    g0_out,
    slab_out,
    slab_qkv,
    small,
    starts,
    near_c,
    near_x,
    tile_own,
    tile_f,
    vec,
    bias_q,
    bias_u,
    wide1,
    normed1,
    gwide,
    wide2,
    gawide,
    unit1,
    unit2,
    inv1,
    inv2,
    r1,
    g1,
    qkv_out,
    qkv_in,
    q_t,
    k_t,
    v_t,
    k_n,
    v_n,
    out_t,
    lse,
    mix_t,
    mixrows_t,
    upre,
    act,
    gp16,
    part_g2,
    via_g2,
    in_g2,
    part_dn,
    via_dn,
    in_dn,
    part_g1,
    via_g1,
    in_g1,
    gm_out,
    gm_in,
    gq_t,
    gk_t,
    gv_t,
    gqkv_out,
    gqkv_in,
    gqkv,
    grads,
    core_in,
    a_via,
    b_via,
    a_in,
    b_in,
    a_sum,
    b_sum,
    a_lastvia,
    b_lastvia,
    a_last,
    b_last,
    vsum,
    tsum,
    s_out,
    s_in,
    s_g,
    sg_c,
    sg_x,
    send_sems,
    recv_sems,
    local_sems,
):
    f, k, t = lax.axis_index("fsdp"), lax.axis_index("ctx"), lax.axis_index("tp")
    z, yh = f // 2, lax.rem(f, 2)
    yl, c = k // 2, lax.rem(k, 2)
    y = yh * 2 + yl
    head = t * 4 + k
    place = f * 4 + k
    slope = jnp.exp2(jnp.full((1, BLOCK), -8.0 / H, F32) * (head + 1).astype(F32))

    def at_zy(zz, yy, cc):
        return (zz * 2 + yy // 2, lax.rem(yy, 2) * 2 + cc, t)

    y_peers = [at_zy(z, around(y, d), c) for d in STEPS]
    z_peers = [at_zy(around(z, d), y, c) for d in STEPS]
    sibling = at_zy(z, y, 1 - c)
    ctx_peers = [(f, around(k, d), t) for d in STEPS]
    fsdp_peers = [(lax.rem(f + d, 8), k, t) for d in range(1, 8)]
    tp_peers = [(f, k, around(t, d)) for d in STEPS]
    group = [(dt, dk) for dt in range(4) for dk in range(4) if (dt, dk) != (0, 0)]

    def member(dt, dk):
        return (f, around(k, dk), around(t, dt))

    def move(index, src, dst):
        copy = pltpu.make_async_copy(src, dst, local_sems.at[index])
        copy.start()
        return copy

    own_out = pl.ds(pl.multiple_of(2816 + t * 256, 256), 256)
    qkv_load = move(0, w_qkv_hbm, w_qkv)
    out_load = move(1, w_out.at[0], whole.at[z, y, c, :, own_out])
    hidden_load = move(2, hidden_hbm, hidden)
    mlp_loads = [
        move(3, w_up.at[0], whole.at[z, y, c, :, 768:1792]),
        move(4, w_down.at[0], whole.at[z, y, c, :, 1792:2816]),
    ]
    cot_load = move(5, cot_hbm, cot)

    barrier = pltpu.get_barrier_semaphore()
    greeted = [member(dt, dk) for dt, dk in group] + y_peers + fsdp_peers
    for partner in greeted:
        pl.semaphore_signal(barrier, inc=1, device_id=partner, device_id_type=MESH)

    def lanes(count, period, index):
        row = lax.broadcasted_iota(jnp.int32, (count, 128), 0)
        lane = lax.broadcasted_iota(jnp.int32, (count, 128), 1)
        return ((lane % count == row) & ((lane % period) // count == index)).astype(F32)

    def scatter(values, hot):
        return lax.dot_general(
            values.astype(F32), hot, NN, precision=lax.Precision.HIGHEST, preferred_element_type=F32
        )

    small[...] = jnp.zeros_like(small)
    own = lanes(8, 128, k * 4 + t)
    small[0:2] = scatter(gain_in[0], own)
    small[2:4] = scatter(shift_in[0], own)
    small[4:6] = scatter(obias_in[0], own)
    pair = lanes(2, 64, place)
    left = lax.broadcasted_iota(jnp.int32, (4, 128), 1) < 64
    q_row, v_row = scatter(qv_in[0, 0], pair), scatter(qv_in[0, 1], pair)
    q_left, q_right = jnp.where(left, q_row, 0.0), jnp.where(left, 0.0, q_row)
    v_left, v_right = jnp.where(left, v_row, 0.0), jnp.where(left, 0.0, v_row)
    small[8:9] = q_left[0:1]
    small[9:10] = v_left[0:1] + q_right[1:2]
    small[10:11] = v_right[1:2]
    small[11:12] = q_left[2:3]
    small[12:13] = v_left[2:3] + q_right[3:4]
    small[13:14] = v_right[3:4]
    up_row = scatter(ub_in[0], lanes(8, 128, lax.rem(place, 16)))
    even = (place < 16).astype(F32)
    for i in range(4):
        small[14 + 2 * i : 15 + 2 * i] = up_row[i : i + 1] * even
        small[15 + 2 * i : 16 + 2 * i] = up_row[i : i + 1] * (1.0 - even)
    qkv_load.wait()
    for j in range(4):
        for i in range(3):
            col = j * 192 + i * 64
            whole[z, y, c, :, col : col + 64] = w_qkv[0, i, :, j * 64 : j * 64 + 64]

    hidden_load.wait()
    r = hidden[...].astype(F32)
    centered = r - row_mean(r)
    rstd = lax.rsqrt(row_mean(centered * centered) + EPS)
    unit1[...] = centered * rstd
    inv1[...] = rstd
    wide1[t] = unit1[...].astype(BF16)
    out_load.wait()

    pl.semaphore_wait(barrier, len(greeted))
    copies = Copies(send_sems, recv_sems)
    make = copies.make
    small_c = [make(small, near_c.at[d - 1], ctx_peers[d - 1]) for d in STEPS]
    far = [(dt, dk) for dt, dk in group if dt]
    small_x = [
        make(small.at[pl.ds(0, 8)], near_x.at[i], member(dt, dk)) for i, (dt, dk) in enumerate(far)
    ]

    upper, lower = pl.ds(0, 16), pl.ds(16, 16)
    low, high = pl.ds(0, 2), pl.ds(2, 2)

    def ring(part, me, peers):
        plus, minus = peers[0], peers[2]
        u, v = part(me)
        plus_u, minus_v = make(u, u, plus), make(v, v, minus)
        plus_v, minus_u = make(v, v, plus), make(u, u, minus)

        def forward():
            plus_u.wait_recv()
            u = part(around(me, 3))[0]
            next_u = make(u, u, plus)
            minus_v.wait_recv()
            v = part(around(me, 1))[1]
            return [plus_v, minus_u, next_u, make(v, v, minus)]

        return forward

    def ring_rows(buffer):
        return ring(
            lambda o: (buffer.at[o, :, pl.ds(0, 512)], buffer.at[o, :, pl.ds(512, 512)]),
            t,
            tp_peers,
        )

    def ring_sum(part, via, land, me, peers, filled=None):
        plus, minus = peers[0], peers[2]
        one, two, three = around(me, 1), around(me, 2), around(me, 3)
        if filled:
            filled(0)
        via_u = make(part(two)[0], via[0], plus)
        near_u = make(part(three)[0], land[1][0], minus)
        if filled:
            filled(1)
        via_v = make(part(two)[1], via[1], minus)
        near_v = make(part(one)[1], land[0][1], plus)
        yield
        via_u.wait_recv()
        via[0][...] = (via[0][...].astype(F32) + part(one)[0][...].astype(F32)).astype(BF16)
        next_u = make(via[0], land[0][0], plus)
        via_v.wait_recv()
        via[1][...] = (via[1][...].astype(F32) + part(three)[1][...].astype(F32)).astype(BF16)
        next_v = make(via[1], land[1][1], minus)
        yield
        arrived([near_u, near_v, next_u, next_v])

    def ring_sum_rows(part, via, land, filled=None):
        ends = pl.ds(0, 512), pl.ds(512, 512)
        return ring_sum(
            lambda o: tuple(part.at[o, :, end] for end in ends),
            (via.at[0], via.at[1]),
            tuple(tuple(land.at[i, :, end] for end in ends) for i in range(2)),
            t,
            tp_peers,
            filled,
        )

    def gather(cols):
        middle = (cols.start + cols.stop) // 2
        ends = slice(cols.start, middle), slice(middle, cols.stop)
        a = ring(lambda o: tuple(whole.at[z, o, c, upper, end] for end in ends), y, y_peers)
        b = ring(lambda o: tuple(whole.at[o, y, c, lower, end] for end in ends), z, z_peers)
        yield
        a, b = a(), b()
        yield
        arrived(a)
        a = ring(lambda o: tuple(whole.at[o, yy, c, upper, cols] for yy in (low, high)), z, z_peers)
        arrived(b)
        b = ring(lambda o: tuple(whole.at[zz, o, c, lower, cols] for zz in (low, high)), y, y_peers)

        def both(d):
            for block in (
                whole.at[around(z, d), :, c, upper, cols],
                whole.at[:, around(y, d), c, lower, cols],
            ):
                core.append(make(block, block, sibling))

        core = []
        both(0)
        yield
        a, b = a(), b()
        yield
        arrived(a + b)
        for d in STEPS:
            both(d)
        yield
        arrived(core)

    gather_qkv = gather(QKV)
    step(gather_qkv)
    wide1_x = ring_rows(wide1)
    out_cols = whole.at[z, y, c, :, own_out]
    out_x = [make(out_cols, out_cols, peer) for peer in tp_peers]

    arrived(small_c)
    arrived(small_x)
    total = small[...] + near_c[0] + near_c[1] + near_c[2]
    norms = total[0:8]
    for i in range(12):
        norms = norms + near_x[i]
    tile_own[0:8] = norms
    tile_own[8:24] = total[8:24]
    small_f = [make(tile_own, tile_f.at[d], fsdp_peers[d]) for d in range(7)]
    step(gather_qkv)
    wide1_x = wide1_x()
    step(gather_qkv)
    arrived(small_f)
    vec[:, pl.ds(pl.multiple_of(f * 128, 128), 128)] = tile_own[0:8]
    columns = tile_own[8:24]
    for d in range(7):
        origin = lax.rem(f + 7 - d, 8)
        vec[:, pl.ds(pl.multiple_of(origin * 128, 128), 128)] = tile_f[d, 0:8]
        columns = columns + tile_f[d, 8:24]
    for i in range(6):
        bias_q[:, i * 128 : (i + 1) * 128] = columns[i : i + 1]
    for i in range(8):
        bias_u[:, i * 128 : (i + 1) * 128] = columns[6 + i : 7 + i]
    cot_load.wait()
    gwide[t] = cot[...].astype(BF16)
    ids = segments[...]
    first = jnp.zeros((1, 2048), F32)
    for value in range(1, 4):
        count = jnp.sum((ids < value).astype(F32), axis=1, keepdims=True)
        first = jnp.where(ids >= value, count, first)
    starts[...] = first
    step(gather_qkv)
    arrived(out_x)
    gather_out = gather(OUT)
    step(gather_out)
    arrived(wide1_x)
    gwide_x = ring_rows(gwide)
    for i in range(4):
        normed1[i] = (wide1[i].astype(F32) * vec[0:1] + vec[2:3]).astype(BF16)
    step(gather_qkv)
    step(gather_out)
    step(gather_qkv)

    def project(n, carry):
        cols = pl.ds(pl.multiple_of(n * 256, 256), 256)
        out = dot(normed1[...].reshape(512, 1024), whole[:, :, :, :, cols].reshape(1024, 256))
        qkv_out[cols] = (out + bias_q[:, cols]).T.astype(BF16)
        return carry

    lax.fori_loop(0, 3, project, 0)

    def head_rows(j):
        return pl.ds(pl.multiple_of(j * 192, 64), 192)

    heads_c = [
        make(qkv_out.at[head_rows(around(k, d))], qkv_in.at[k], ctx_peers[d - 1]) for d in STEPS
    ]
    qkv_in[k] = qkv_out[head_rows(k)]
    step(gather_out)
    gwide_x = gwide_x()
    step(gather_out)
    arrived(heads_c)
    for copy in mlp_loads:
        copy.wait()
    gather_mlp = gather(MLP)
    step(gather_mlp)
    for i in range(4):
        span = slice(i * 512, (i + 1) * 512)
        q_t[:, span] = qkv_in[i, 0:64]
        keys = qkv_in[i, 64:128]
        values = qkv_in[i, 128:192]
        k_t[:, span] = keys
        v_t[:, span] = values
        k_n[span] = keys.T
        v_n[span] = values.T

    def scores(first, begin, width):
        at = pl.ds(first, BLOCK)
        s = dot(k_n[pl.ds(begin, width)], q_t[:, at])
        key = begin + lax.broadcasted_iota(jnp.int32, (width, BLOCK), 0)
        query = first + lax.broadcasted_iota(jnp.int32, (width, BLOCK), 1)
        s = s * 0.125 + slope * (key - first).astype(F32)
        return jnp.where((key <= query) & (key.astype(F32) >= starts[:, at]), s, -jnp.inf)

    def attend(first, begin, width):
        at = pl.ds(first, BLOCK)
        s = scores(first, begin, width)
        highest = jnp.max(s, axis=0, keepdims=True)
        e = jnp.exp(s - highest)
        totals = jnp.sum(e, axis=0, keepdims=True)
        probs = (e * (1.0 / totals)).astype(BF16)
        out_t[:, at] = dot(v_t[:, pl.ds(begin, width)], probs).astype(BF16)
        lse[:, at] = highest + jnp.log(totals)

    def blocks(body, *between):
        def later(b, carry):
            begin = pl.multiple_of(b * BLOCK, BLOCK)
            body(pl.multiple_of(begin + 1024, BLOCK), begin, 1024 + BLOCK)
            return carry

        for b in range(4):
            body(b * BLOCK, 0, (b + 1) * BLOCK)
            if b == 1:
                between[0]()
        between[1]()
        lax.fori_loop(0, 2, later, 0)
        between[2]()
        lax.fori_loop(2, 4, later, 0)
        between[3]()

    blocks(
        attend,
        lambda: step(gather_out, gather_mlp),
        lambda: step(gather_mlp),
        lambda: step(gather_mlp),
        lambda: None,
    )

    def own_lanes(kk, tt):
        return pl.ds(pl.multiple_of(kk * 512 + tt * 128, 128), 128)

    mine_rows = pl.ds(pl.multiple_of(head * 64, 64), 64)
    mix_g = [
        make(out_t.at[:, own_lanes(around(k, dk), around(t, dt))], mix_t.at[mine_rows], member(dt, dk))
        for dt, dk in group
    ]
    mix_t[mine_rows] = out_t[:, own_lanes(k, t)]
    step(gather_out, gather_mlp)
    arrived(mix_g)
    local_rows = pl.ds(pl.multiple_of(k * 64, 64), 64)
    mixrows_c = [
        make(
            out_t.at[:, pl.ds(pl.multiple_of(around(k, d) * 512, 512), 512)],
            mixrows_t.at[local_rows],
            ctx_peers[d - 1],
        )
        for d in STEPS
    ]
    mixrows_t[local_rows] = out_t[:, pl.ds(pl.multiple_of(k * 512, 512), 512)]

    for n in range(4):
        cols = slice(n * 256, (n + 1) * 256)
        out = dot(whole[n, :, :, :, OUT].reshape(256, 1024), mix_t[...])
        r1[:, cols] = hidden[:, cols].astype(F32) + out.T + vec[4:5, cols]
    r = r1[...]
    centered = r - row_mean(r)
    rstd = lax.rsqrt(row_mean(centered * centered) + EPS)
    unit2[...] = centered * rstd
    inv2[...] = rstd
    wide2[t] = (unit2[...] * vec[1:2] + vec[3:4]).astype(BF16)
    wide2_x = ring_rows(wide2)
    step(gather_mlp)
    arrived(gwide_x)

    def pull(n, carry):
        cols = pl.ds(pl.multiple_of(n * 256, 256), 256)
        wcols = pl.ds(pl.multiple_of(1792 + n * 256, 256), 256)
        upre[:, cols] = dot(
            gwide[...].reshape(512, 1024), whole[:, :, :, :, wcols].reshape(1024, 256)
        )
        return carry

    lax.fori_loop(0, 2, pull, 0)
    wide2_x = wide2_x()
    lax.fori_loop(2, 4, pull, 0)
    arrived(wide2_x)

    def feed(n, carry):
        cols = pl.ds(pl.multiple_of(n * 256, 256), 256)
        wcols = pl.ds(pl.multiple_of(768 + n * 256, 256), 256)
        pre = (
            dot(wide2[...].reshape(512, 1024), whole[:, :, :, :, wcols].reshape(1024, 256))
            + bias_u[:, cols]
        )
        curve = jnp.tanh(ROOT * (pre + CUBIC * pre * pre * pre))
        act[:, cols] = (0.5 * pre * (1.0 + curve)).astype(BF16)
        slant = 0.5 * (1.0 + curve) + 0.5 * pre * (1.0 - curve * curve) * ROOT * (
            1.0 + 3.0 * CUBIC * pre * pre
        )
        gpre = upre[:, cols] * slant
        gp16[:, cols] = gpre.astype(BF16)
        bias_u[:, cols] = jnp.sum(gpre, axis=0, keepdims=True)
        return carry

    lax.fori_loop(0, 4, feed, 0)

    def partial_rows(source, cols, part):
        def one(n, carry):
            width = cols.stop - cols.start
            out = dot(source[...], whole[n, :, :, :, cols].reshape(256, width), NT)
            part[:, :, pl.ds(pl.multiple_of(n * 256, 256), 256)] = out.astype(BF16).reshape(
                4, 128, 256
            )
            return carry

        return lambda half: lax.fori_loop(2 * half, 2 * half + 2, one, 0)

    def sum_rows(part, landing):
        return part[t].astype(F32) + landing[0].astype(F32) + landing[1].astype(F32)

    sum_g2 = ring_sum_rows(part_g2, via_g2, in_g2, partial_rows(gp16, UP, part_g2))
    step(sum_g2)

    def matrix_grad(left, right, chunk):
        width = CHUNKS[chunk][1]

        def one(m, carry):
            rows = left[:, :, pl.ds(pl.multiple_of(m * 256, 256), 256)].reshape(512, 256)
            out = dot(rows, right[...], TN)
            grads[chunk][m] = out.astype(BF16).reshape(4, 2, 32, width)
            return carry

        lax.fori_loop(0, 4, one, 0)

    def reduce(i):
        offset, width = CHUNKS[i]
        both = core_in[i]
        core = make(grads[i].at[:, :, 1 - c], both, sibling)
        yield
        core.wait_recv()

        def add(j, carry):
            zz, yy = j // 4, lax.rem(j, 4)
            total = grads[i][zz, yy, c].astype(F32) + both[zz, yy].astype(F32)
            both[zz, yy] = total.astype(BF16)
            return carry

        lax.fori_loop(0, 16, add, 0)
        yield
        a = ring_sum(
            lambda o: (both.at[o, low, upper], both.at[o, high, upper]),
            (a_via[i].at[low], a_via[i].at[high]),
            tuple((a_in[i].at[d, low], a_in[i].at[d, high]) for d in range(2)),
            z,
            z_peers,
        )
        b = ring_sum(
            lambda o: (both.at[low, o, lower], both.at[high, o, lower]),
            (b_via[i].at[low], b_via[i].at[high]),
            tuple((b_in[i].at[d, low], b_in[i].at[d, high]) for d in range(2)),
            y,
            y_peers,
        )
        step(a, b)
        yield
        step(a, b)
        yield
        step(a)
        for j in range(4):
            total = both[z, j, 0:16].astype(F32)
            for d in range(2):
                total = total + a_in[i][d, j].astype(F32)
            a_sum[i][j] = total.astype(BF16)
        ends = pl.ds(0, width // 2), pl.ds(width // 2, width // 2)
        a = ring_sum(
            lambda o: tuple(a_sum[i].at[o, :, end] for end in ends),
            tuple(a_lastvia[i].at[:, end] for end in ends),
            tuple(tuple(a_last[i].at[d, :, end] for end in ends) for d in range(2)),
            y,
            y_peers,
        )
        step(a)
        step(b)
        for j in range(4):
            total = both[j, y, 16:32].astype(F32)
            for d in range(2):
                total = total + b_in[i][d, j].astype(F32)
            b_sum[i][j] = total.astype(BF16)
        b = ring_sum(
            lambda o: tuple(b_sum[i].at[o, :, end] for end in ends),
            tuple(b_lastvia[i].at[:, end] for end in ends),
            tuple(tuple(b_last[i].at[d, :, end] for end in ends) for d in range(2)),
            z,
            z_peers,
        )
        step(b)
        yield
        step(a, b)
        yield
        step(a, b)
        cols = slice(offset, offset + width)
        slab_out[0:16, cols] = (
            a_sum[i][y].astype(F32) + a_last[i][0].astype(F32) + a_last[i][1].astype(F32)
        )
        slab_out[16:32, cols] = (
            b_sum[i][z].astype(F32) + b_last[i][0].astype(F32) + b_last[i][1].astype(F32)
        )

    matrix_grad(wide2, gp16, 0)
    reduce_up = reduce(0)
    step(reduce_up, sum_g2)
    down_rows = partial_rows(act, DOWN, part_dn)
    down_rows(0)
    down_rows(1)
    matrix_grad(gwide, act, 1)
    reduce_down = reduce(1)
    step(reduce_down)

    def norm_back(total, unit, inv, gain):
        scaled = total * gain
        return inv * (scaled - row_mean(scaled) - unit * row_mean(scaled * unit))

    step(sum_g2)
    total = sum_rows(part_g2, in_g2)
    vsum[1:2] = jnp.sum(total * unit2[...], axis=0, keepdims=True)
    vsum[3:4] = jnp.sum(total, axis=0, keepdims=True)
    vsum[5:6] = jnp.sum(cot[...], axis=0, keepdims=True)
    grad_mid = cot[...] + norm_back(total, unit2[...], inv2[...], vec[1:2])
    g1[...] = grad_mid
    vsum[4:5] = jnp.sum(grad_mid, axis=0, keepdims=True)
    gawide[t] = grad_mid.astype(BF16)
    for n in range(4):
        cols = slice(n * 256, (n + 1) * 256)
        wcols = slice(2816 + n * 256, 2816 + (n + 1) * 256)
        out = dot(gawide[t], whole[:, :, :, :, wcols].reshape(1024, 256))
        gm_out[cols] = out.T.astype(BF16)
    gm_g = [
        make(
            gm_out.at[
                pl.ds(pl.multiple_of((around(t, dt) * 4 + around(k, dk)) * 64, 64), 64)
            ],
            gm_in.at[:, own_lanes(k, t)],
            member(dt, dk),
        )
        for dt, dk in group
    ]
    gm_in[:, own_lanes(k, t)] = gm_out[mine_rows]
    step(reduce_up, reduce_down)
    arrived(gm_g)
    gawide_x = ring_rows(gawide)
    step(reduce_up)
    gk_t[...] = jnp.zeros_like(gk_t)
    gv_t[...] = jnp.zeros_like(gv_t)

    def attend_back(first, begin, width):
        at = pl.ds(first, BLOCK)
        window = pl.ds(begin, width)
        p = jnp.exp(scores(first, begin, width) - lse[:, at])
        grad = gm_in[:, at]
        gv_t[:, window] += dot(grad, p.astype(BF16), NT)
        dp = dot(v_n[window], grad)
        centre = jnp.sum(p * dp, axis=0, keepdims=True)
        ds = (p * (dp - centre) * 0.125).astype(BF16)
        gq_t[:, at] = dot(k_t[:, window], ds).astype(BF16)
        gk_t[:, window] += dot(q_t[:, at], ds, NT)

    sum_dn = ring_sum_rows(part_dn, via_dn, in_dn)
    waiting = []

    def second():
        step(reduce_up, reduce_down)
        waiting.append(gawide_x())
        step(sum_dn)

    blocks(
        attend_back,
        second,
        lambda: step(reduce_up, reduce_down, sum_dn),
        lambda: step(reduce_up, reduce_down, sum_dn),
        lambda: None,
    )
    gawide_x = waiting[0]
    for j in range(4):
        span = slice(j * 512, (j + 1) * 512)
        gqkv_out[j, 0:64] = gq_t[:, span]
        gqkv_out[j, 64:128] = gk_t[:, span].astype(BF16)
        gqkv_out[j, 128:192] = gv_t[:, span].astype(BF16)
    back_c = [
        make(gqkv_out.at[around(k, d)], gqkv_in.at[k], ctx_peers[d - 1]) for d in STEPS
    ]
    gqkv_in[k] = gqkv_out[k]
    arrived(gawide_x)
    arrived(mixrows_c)
    gp16[:, 0:256] = mixrows_t[...].T
    matrix_grad(gawide, gp16.at[:, pl.ds(0, 256)], 2)
    reduce_out = reduce(2)
    step(reduce_out, reduce_up, reduce_down)
    r2_out[...] = r1[...] + sum_rows(part_dn, in_dn) + vec[5:6]
    stores = [move(6, r2_out, r2_hbm)]
    arrived(back_c)
    gqkv[...] = gqkv_in[...].reshape(768, 512).T
    sum_g1 = ring_sum_rows(part_g1, via_g1, in_g1, partial_rows(gqkv, QKV, part_g1))
    step(sum_g1)
    step(reduce_out, reduce_down)
    sums = jnp.sum(gqkv[...].astype(F32), axis=0, keepdims=True)
    for i in range(6):
        tsum[i : i + 1] = sums[:, i * 128 : (i + 1) * 128]
    for i in range(8):
        tsum[6 + i : 7 + i] = bias_u[:, i * 128 : (i + 1) * 128]
    tsum[14:16] = jnp.zeros((2, 128), F32)
    matrix_grad(normed1, gqkv, 3)
    reduce_qkv = reduce(3)
    step(reduce_qkv, sum_g1, reduce_out)

    step(reduce_qkv)
    step(reduce_qkv)
    step(sum_g1)
    total = sum_rows(part_g1, in_g1)
    vsum[0:1] = jnp.sum(total * unit1[...], axis=0, keepdims=True)
    vsum[2:3] = jnp.sum(total, axis=0, keepdims=True)
    vsum[6:8] = jnp.zeros((2, 1024), F32)
    for i in range(8):
        s_out[i, 0:8] = vsum[:, i * 128 : (i + 1) * 128]
        s_out[i, 8:24] = tsum[...]
    sum_f = [
        make(s_out.at[lax.rem(f + d + 1, 8)], s_in.at[d], fsdp_peers[d]) for d in range(7)
    ]
    step(reduce_qkv, reduce_out)
    g0_out[...] = g1[...] + norm_back(total, unit1[...], inv1[...], vec[0:1])
    stores.append(move(7, g0_out, g0_hbm))
    step(reduce_qkv, reduce_out)
    arrived(sum_f)
    total = s_out[f]
    for d in range(7):
        total = total + s_in[d]
    s_g[...] = total
    sum_c = [make(s_g, sg_c.at[d - 1], ctx_peers[d - 1]) for d in STEPS]
    sum_x = [
        make(s_g.at[pl.ds(0, 8)], sg_x.at[i], member(dt, dk)) for i, (dt, dk) in enumerate(far)
    ]
    step(reduce_qkv, reduce_out)
    step(reduce_qkv, reduce_out)
    step(reduce_up, reduce_down)
    for j in range(4):
        for i in range(3):
            col = 2048 + j * 192 + i * 64
            slab_qkv[0, i, :, j * 64 : j * 64 + 64] = slab_out[:, col : col + 64]
    stores += [
        move(8, slab_qkv, qkv_hbm),
        move(9, slab_out.at[:, 2816:3072], out_hbm.at[0]),
        move(10, slab_out.at[:, 0:1024], up_hbm.at[0]),
        move(11, slab_out.at[:, 1024:2048], down_hbm.at[0]),
    ]
    arrived(sum_c)
    arrived(sum_x)
    total = s_g[...] + sg_c[0] + sg_c[1] + sg_c[2]
    norms = total[0:8]
    for i in range(12):
        norms = norms + sg_x[i]
    def pick(values, hot):
        return lax.dot_general(
            values, hot, NT, precision=lax.Precision.HIGHEST, preferred_element_type=F32
        )

    mine = pick(norms, own)
    gain_out[0] = mine[0:2]
    shift_out[0] = mine[2:4]
    obias_out[0] = mine[4:6]
    left = lax.broadcasted_iota(jnp.int32, (2, 128), 1) < 64
    from_left = pick(total[8:24], jnp.where(left, pair, 0.0))
    from_right = pick(total[8:24], jnp.where(left, 0.0, pair))
    qv_out[0, 0, 0:1] = from_left[0:1]
    qv_out[0, 0, 1:2] = from_right[1:2]
    qv_out[0, 0, 2:3] = from_left[3:4]
    qv_out[0, 0, 3:4] = from_right[4:5]
    qv_out[0, 1, 0:1] = from_left[1:2]
    qv_out[0, 1, 1:2] = from_right[2:3]
    qv_out[0, 1, 2:3] = from_left[4:5]
    qv_out[0, 1, 3:4] = from_right[5:6]
    ups = pick(total[8:24], lanes(8, 128, lax.rem(place, 16)))
    for i in range(4):
        ub_out[0, i : i + 1] = (
            ups[6 + 2 * i : 7 + 2 * i] * even + ups[7 + 2 * i : 8 + 2 * i] * (1.0 - even)
        )
    for copy in stores:
        copy.wait()
    copies.finish()


def place_kernel(*refs):
    count = len(refs) // 2
    for src, dst in zip(refs[:count], refs[count:]):
        dst[...] = src[...]


OUTPUTS = (
    (128, 1024),
    (128, 1024),
    (1, 3, 32, 256),
    (1, 32, 256),
    (1, 32, 1024),
    (1, 32, 1024),
    (1, 2, 8),
    (1, 2, 8),
    (1, 2, 8),
    (1, 2, 4, 2),
    (1, 4, 8),
)
COUNT = 336


def run_layer(*operands):
    vmem = pltpu.VMEM

    def per_chunk(*shape):
        return tuple(vmem((*shape, width), BF16) for _, width in CHUNKS)

    scratch = [
        vmem((4, 4, 2, 32, WIDE), BF16),
        vmem((1, 3, 32, 256), BF16),
        vmem((128, 1024), BF16),
        vmem((128, 1024), F32),
        vmem((128, 1024), F32),
        vmem((128, 1024), F32),
        vmem((32, SLAB), F32),
        vmem((1, 3, 32, 256), F32),
        vmem((24, 128), F32),
        vmem((1, 2048), F32),
        vmem((3, 24, 128), F32),
        vmem((12, 8, 128), F32),
        vmem((24, 128), F32),
        vmem((7, 24, 128), F32),
        vmem((8, 1024), F32),
        vmem((1, 768), F32),
        vmem((1, 1024), F32),
        vmem((4, 128, 1024), BF16),
        vmem((4, 128, 1024), BF16),
        vmem((4, 128, 1024), BF16),
        vmem((4, 128, 1024), BF16),
        vmem((4, 128, 1024), BF16),
        vmem((128, 1024), F32),
        vmem((128, 1024), F32),
        vmem((128, 1), F32),
        vmem((128, 1), F32),
        vmem((128, 1024), F32),
        vmem((128, 1024), F32),
        vmem((768, 512), BF16),
        vmem((4, 192, 512), BF16),
        vmem((64, 2048), BF16),
        vmem((64, 2048), BF16),
        vmem((64, 2048), BF16),
        vmem((2048, 64), BF16),
        vmem((2048, 64), BF16),
        vmem((64, 2048), BF16),
        vmem((1, 2048), F32),
        vmem((1024, 128), BF16),
        vmem((256, 512), BF16),
        vmem((512, 1024), F32),
        vmem((512, 1024), BF16),
        vmem((512, 1024), BF16),
        vmem((4, 128, 1024), BF16),
        vmem((2, 128, 512), BF16),
        vmem((2, 128, 1024), BF16),
        vmem((4, 128, 1024), BF16),
        vmem((2, 128, 512), BF16),
        vmem((2, 128, 1024), BF16),
        vmem((4, 128, 1024), BF16),
        vmem((2, 128, 512), BF16),
        vmem((2, 128, 1024), BF16),
        vmem((1024, 128), BF16),
        vmem((64, 2048), BF16),
        vmem((64, 2048), BF16),
        vmem((64, 2048), F32),
        vmem((64, 2048), F32),
        vmem((4, 192, 512), BF16),
        vmem((4, 192, 512), BF16),
        vmem((512, 768), BF16),
        per_chunk(4, 4, 2, 32),
        per_chunk(4, 4, 32),
        per_chunk(4, 16),
        per_chunk(4, 16),
        per_chunk(2, 4, 16),
        per_chunk(2, 4, 16),
        per_chunk(4, 16),
        per_chunk(4, 16),
        per_chunk(16),
        per_chunk(16),
        per_chunk(2, 16),
        per_chunk(2, 16),
        vmem((8, 1024), F32),
        vmem((16, 128), F32),
        vmem((8, 24, 128), F32),
        vmem((7, 24, 128), F32),
        vmem((24, 128), F32),
        vmem((3, 24, 128), F32),
        vmem((12, 8, 128), F32),
        pltpu.SemaphoreType.DMA((COUNT,)),
        pltpu.SemaphoreType.DMA((COUNT,)),
        pltpu.SemaphoreType.DMA((12,)),
    ]
    in_vmem, in_place = pl.BlockSpec(memory_space=pltpu.VMEM), pl.BlockSpec(memory_space=pl.ANY)
    shapes = tuple(jax.ShapeDtypeStruct(shape, F32) for shape in OUTPUTS)
    places = (in_place,) * 6 + (in_vmem,) * 5
    results = pl.pallas_call(
        layer_kernel,
        out_shape=shapes,
        in_specs=[in_place] * 4 + [in_vmem] * 5 + [in_place] * 2 + [in_vmem],
        out_specs=places,
        scratch_shapes=scratch,
        compiler_params=pltpu.CompilerParams(
            collective_id=0, has_side_effects=True, vmem_limit_bytes=60 << 20
        ),
        name="layer",
    )(*operands)
    return pl.pallas_call(
        place_kernel,
        out_shape=shapes,
        in_specs=[in_vmem] * len(shapes),
        out_specs=(in_vmem,) * len(shapes),
        name="place",
    )(*results)


def on_device(
    hidden_in,
    segment_ids,
    norm_gain,
    norm_bias,
    w_qkv,
    qv_bias,
    w_out,
    out_bias,
    w_up,
    up_bias,
    w_down,
    cotangent,
):
    hidden_out, grad_input, qkv, out, up, down, gain, shift, obias, qv, ub = run_layer(
        w_up,
        w_down,
        w_qkv,
        w_out,
        norm_gain,
        norm_bias,
        out_bias,
        qv_bias,
        up_bias,
        hidden_in,
        cotangent,
        segment_ids,
    )
    return hidden_out, grad_input, gain, shift, qkv, qv, out, obias, up, ub, down


def solution(mesh):
    return jax.shard_map(
        on_device,
        mesh=mesh,
        in_specs=(
            P(("fsdp", "ctx", "tp"), None),
            P("fsdp", None),
            P(None, None, ("fsdp", "ctx", "tp")),
            P(None, None, ("fsdp", "ctx", "tp")),
            P(None, None, ("fsdp", "ctx"), "tp"),
            P(None, None, "tp", ("fsdp", "ctx")),
            P(None, ("fsdp", "ctx"), "tp"),
            P(None, None, ("fsdp", "ctx", "tp")),
            P(None, ("fsdp", "ctx"), "tp"),
            P(None, "tp", ("fsdp", "ctx")),
            P(None, ("fsdp", "ctx"), "tp"),
            P(("fsdp", "ctx", "tp"), None),
        ),
        out_specs=(
            P(("fsdp", "ctx", "tp"), None),
            P(("fsdp", "ctx", "tp"), None),
            P(None, None, ("fsdp", "ctx", "tp")),
            P(None, None, ("fsdp", "ctx", "tp")),
            P(None, None, ("fsdp", "ctx"), "tp"),
            P(None, None, "tp", ("fsdp", "ctx")),
            P(None, ("fsdp", "ctx"), "tp"),
            P(None, None, ("fsdp", "ctx", "tp")),
            P(None, ("fsdp", "ctx"), "tp"),
            P(None, "tp", ("fsdp", "ctx")),
            P(None, ("fsdp", "ctx"), "tp"),
        ),
        check_vma=False,
    )
```
